256 devices in a mesh: seq: 16 (over z, y_lo), head: 16 (over x, y_hi, core).
Axes of the slice: x: 4, y: 4 (y_hi: 2, y_lo: 2; y = y_hi * 2 + y_lo), z: 8, core: 2. Of those that a mesh axis runs over, the one named last changes fastest.
Arguments:
- cache: bfloat16 [2048, 576], P('seq'), may hold values from -8 to 8
- query_nope: bfloat16 [2048, 16384], P('seq', 'head'), may hold values from -5 to 5
- query_rope: bfloat16 [2048, 8192], P('seq', 'head'), may hold values from -256 to 256
- scale_exp: int32 [2048], P('seq'), may hold values from -1 to 1
- offsets: int32 [32], P('seq'), may hold values from 0 to 1984
- up_key: bfloat16 [512, 16384], P(None, 'head'), may hold values from -0.25 to 0.25
- up_value: bfloat16 [512, 16384], P(None, 'head'), may hold values from -0.25 to 0.25
- grad_out: bfloat16 [2048, 16384], P('seq', 'head'), may hold values from -5 to 5
Outputs:
- d_cache: bfloat16 [2048, 576], P('seq')
- d_query_nope: bfloat16 [2048, 16384], P('seq', 'head')
- d_query_rope: bfloat16 [2048, 8192], P('seq', 'head')
The draws below stay inside these ranges and needn't reach their ends.
All inputs are finite; a program needn't handle non-finite values.
Results may differ from the reference program's by a relative error of at most 0.0099.
Values may be sent and summed in bfloat16 or wider, within the bound.
No kernel may reach another device: no remote copies, remote signals or barrier semaphores. Data moves between devices by JAX's collectives and lax.ppermute only.
A program may use at most 64 MiB of HBM per device.

```python
import jax
import jax.numpy as jnp
from jax import lax

LATENT = 512
ROPE = 64
NOPE = 128
QBLOCK = 64
HEADS = 128
QUERIES = 2048
KEYS = 2048


def shared_draw(key):
    base = jax.random.fold_in(key, 4049)
    exponents = jax.random.randint(jax.random.fold_in(base, 1), (QUERIES,), -1, 2).astype(jnp.int32)
    return exponents


def draw_scale_exp(key, part):
    exponents = shared_draw(key)
    return exponents


def draw_cache(key, part):
    first = jax.random.fold_in(key, 17)
    latent = jnp.clip(jax.random.normal(jax.random.fold_in(first, 4), (KEYS, LATENT), jnp.float32), -4.0, 4.0)
    rotary = jnp.clip(jax.random.normal(jax.random.fold_in(first, 5), (KEYS, ROPE), jnp.float32), -4.0, 4.0)
    return jnp.concatenate([latent, rotary], axis=1).astype(jnp.bfloat16)


def draw_query_rope(key, part):
    first = jax.random.fold_in(key, 29)
    values = jnp.clip(jax.random.normal(jax.random.fold_in(first, 2), (QUERIES, HEADS * ROPE), jnp.float32), -4.0, 4.0)
    return values.astype(jnp.bfloat16)


def set_ends(array, own_key, least, top_value):
    longest = array.shape.index(max(array.shape))
    spots = []
    for shift in (0, 1):
        where = [jax.random.randint(jax.random.fold_in(own_key, axis), (), 0, length) for axis, length in enumerate(array.shape)]
        where[longest] = (where[longest] + shift) % array.shape[longest]
        spots.append(tuple(where))
    return array.at[spots[0]].set(least).at[spots[1]].set(top_value)


def steps_of(rng, dims, cuts, least, top_value):
    factor_of = 1.0
    for position, blocks in cuts:
        heights = jax.random.uniform(jax.random.fold_in(jax.random.fold_in(rng, 6), position), (blocks,), jnp.float32, least / len(cuts), top_value / len(cuts))
        factor_of = factor_of * jnp.repeat(jnp.exp(heights), dims[position] // blocks).reshape((-1,) + (1,) * (len(dims) - 1 - position))
    return factor_of


def normal_values(key, extent, spread, bound, pieces=(), kind=jnp.bfloat16):
    entries = jax.random.normal(key, extent, jnp.float32) * spread
    if len(pieces) > 0:
        entries = steps_of(key, extent, pieces, -0.22, 0.18) * entries
    return jnp.clip(entries, min=-bound, max=bound).astype(kind)


def setup_inputs(seed: int = 0) -> dict:
    splits = jax.random.split(jax.random.key(seed), 9)
    cache = draw_cache(jax.random.fold_in(splits[8], 71), 0)
    query_nope = normal_values(splits[1], (QUERIES, HEADS * NOPE), 1.0, 5.0, ((0, 16), (1, 16)))
    query_rope = draw_query_rope(jax.random.fold_in(splits[8], 71), 0)
    scale_exp = draw_scale_exp(jax.random.fold_in(splits[8], 71), 0)
    offsets = set_ends(jax.random.randint(splits[4], (QUERIES // QBLOCK,), 0, KEYS - QBLOCK + 1), jax.random.fold_in(splits[4], 1), 0, KEYS - QBLOCK).astype(jnp.int32)
    up_key = normal_values(splits[5], (LATENT, HEADS * NOPE), LATENT ** -0.5, 0.25, ((1, 16),))
    up_value = normal_values(splits[6], (LATENT, HEADS * NOPE), LATENT ** -0.5, 0.25, ((1, 16),))
    grad_out = normal_values(splits[7], (QUERIES, HEADS * NOPE), 1.0, 5.0, ((0, 16), (1, 16)))
    return dict(cache=cache, query_nope=query_nope, query_rope=query_rope, scale_exp=scale_exp, offsets=offsets, up_key=up_key, up_value=up_value, grad_out=grad_out)


def reference(cache, query_nope, query_rope, scale_exp, offsets, up_key, up_value, grad_out):
    scale = (NOPE + ROPE) ** -0.5
    factor = jnp.exp2(scale_exp.astype(jnp.float32))[:, None]
    q_nope = (query_nope.astype(jnp.float32) * factor).astype(jnp.bfloat16).reshape(QUERIES, HEADS, NOPE)
    q_rope = (query_rope.astype(jnp.float32) * factor).astype(jnp.bfloat16).reshape(QUERIES, HEADS, ROPE)
    outgrad = grad_out.reshape(QUERIES, HEADS, NOPE)
    w_key = up_key.reshape(LATENT, HEADS, NOPE)
    w_value = up_value.reshape(LATENT, HEADS, NOPE)
    positions = (offsets[:, None] + jnp.arange(QBLOCK, dtype=jnp.int32)[None, :]).reshape(-1)
    visible = jnp.arange(KEYS, dtype=jnp.int32)[None, :] <= positions[:, None]
    latent = cache[:, :LATENT]

    def one_head(total, items):
        head_nope, head_rope, head_key, head_value, head_grad = items
        absorbed = jnp.dot(head_nope, head_key.T, preferred_element_type=jnp.float32).astype(jnp.bfloat16)
        extended = jnp.concatenate([absorbed, head_rope], axis=1)
        back = jnp.dot(head_grad, head_value.T, preferred_element_type=jnp.float32).astype(jnp.bfloat16)
        raw = jnp.dot(extended, cache.T, preferred_element_type=jnp.float32) * scale
        scores = jnp.where(visible, raw, -jnp.inf)
        top = jnp.max(scores, axis=1, keepdims=True)
        lse = top + jnp.log(jnp.sum(jnp.exp(scores - top), axis=1, keepdims=True))
        probs = jnp.exp(scores - lse)
        probs_b = probs.astype(jnp.bfloat16)
        latent_out = jnp.dot(probs_b, latent, preferred_element_type=jnp.float32)
        delta = jnp.sum(back.astype(jnp.float32) * latent_out, axis=1, keepdims=True)
        dprob = jnp.dot(back, latent.T, preferred_element_type=jnp.float32)
        dscore = (probs * (dprob - delta) * scale).astype(jnp.bfloat16)
        grad_ext = jnp.dot(dscore, cache, preferred_element_type=jnp.float32)
        grad_abs = grad_ext[:, :LATENT].astype(jnp.bfloat16)
        dq_nope = jnp.dot(grad_abs, head_key, preferred_element_type=jnp.float32) * factor
        dq_rope = grad_ext[:, LATENT:] * factor
        term = jnp.dot(dscore.T, extended, preferred_element_type=jnp.float32)
        term_value = jnp.dot(probs_b.T, back, preferred_element_type=jnp.float32)
        total = total + term + jnp.pad(term_value, ((0, 0), (0, ROPE)))
        return total, (dq_nope.astype(jnp.bfloat16), dq_rope.astype(jnp.bfloat16))

    items = (jnp.transpose(q_nope, (1, 0, 2)), jnp.transpose(q_rope, (1, 0, 2)),
             jnp.transpose(w_key, (1, 0, 2)), jnp.transpose(w_value, (1, 0, 2)),
             jnp.transpose(outgrad, (1, 0, 2)))
    start = jnp.zeros((KEYS, LATENT + ROPE), jnp.float32)
    total, (dq_nope, dq_rope) = lax.scan(one_head, start, items)
    d_query_nope = jnp.transpose(dq_nope, (1, 0, 2)).reshape(QUERIES, HEADS * NOPE)
    d_query_rope = jnp.transpose(dq_rope, (1, 0, 2)).reshape(QUERIES, HEADS * ROPE)
    return total.astype(jnp.bfloat16), d_query_nope, d_query_rope
```

```python
import jax
import jax.numpy as jnp
from jax import lax
from jax.sharding import Mesh, PartitionSpec as P

LATENT = 512
ROPE = 64
NOPE = 128
QBLOCK = 64
WIDTH = LATENT + ROPE
LANES = 128
ROWS = 16
PACKED = ROWS * WIDTH // LANES
SEQ = ("z", "y_lo")
HEAD = ("x", "y_hi", "core")


def pack_rows(rows):
    latent = rows[:, :LATENT].reshape(ROWS, LATENT // LANES, LANES)
    latent = jnp.transpose(latent, (1, 0, 2)).reshape(-1, LANES)
    rotary = rows[:, LATENT:]
    rotary = jnp.concatenate([rotary[: ROWS // 2], rotary[ROWS // 2 :]], axis=1)
    return jnp.concatenate([latent, rotary], axis=0)


def unpack_rows(packed):
    lead = packed.shape[:-2]
    latent = packed[..., : ROWS * LATENT // LANES, :].reshape(*lead, LATENT // LANES, ROWS, LANES)
    latent = jnp.swapaxes(latent, -3, -2).reshape(*lead, ROWS, LATENT)
    rotary = packed[..., ROWS * LATENT // LANES :, :]
    rotary = jnp.concatenate([rotary[..., :ROPE], rotary[..., ROPE:]], axis=-2)
    return jnp.concatenate([latent, rotary], axis=-1)


def pack_all(rows):
    lead = rows.shape[:-2]
    latent = rows[..., :LATENT].reshape(*lead, ROWS, LATENT // LANES, LANES)
    latent = jnp.swapaxes(latent, -3, -2).reshape(*lead, ROWS * LATENT // LANES, LANES)
    rotary = rows[..., LATENT:]
    rotary = jnp.concatenate([rotary[..., : ROWS // 2, :], rotary[..., ROWS // 2 :, :]], axis=-1)
    return jnp.concatenate([latent, rotary], axis=-2)


def to_each(block, axes):
    copies = jnp.broadcast_to(block, (lax.axis_size(axes), *block.shape))
    return lax.all_to_all(copies, axes, 0, 0, tiled=True)


def swap_core(block):
    return lax.ppermute(block, "core", [(0, 1), (1, 0)])


def add_up(blocks):
    return jnp.sum(blocks.astype(jnp.float32), axis=0).astype(jnp.bfloat16)


def gather_cache(cache):
    own = lax.axis_index(("x", "core"))
    mine = pack_rows(lax.dynamic_slice_in_dim(cache, own * ROWS, ROWS, 0))
    over_seq = to_each(mine, SEQ)
    here = to_each(over_seq, "x")
    there = swap_core(here)
    return here, there


def owned_rows(keep, send):
    half = (keep.astype(jnp.float32) + swap_core(send).astype(jnp.float32)).astype(jnp.bfloat16)
    slices = add_up(lax.all_to_all(half, "x", 0, 0, tiled=True))
    slices = add_up(lax.all_to_all(slices, SEQ, 0, 0, tiled=True))
    parts = to_each(slices, HEAD)
    sizes = [lax.axis_size(axis) for axis in HEAD]
    parts = parts.reshape(*sizes, PACKED, LANES).astype(jnp.float32)
    parts = jnp.sum(parts, axis=1).astype(jnp.bfloat16)
    return unpack_rows(parts).reshape(-1, WIDTH)


def per_device(cache, query_nope, query_rope, scale_exp, offsets, up_key, up_value, grad_out):
    core = lax.axis_index("core")
    here, there = gather_cache(cache)
    both = jnp.stack([jnp.where(core == 0, here, there), jnp.where(core == 0, there, here)])
    whole = jnp.transpose(unpack_rows(both), (2, 1, 0, 3, 4)).reshape(-1, WIDTH)
    keys_total = whole.shape[0]
    queries = query_nope.shape[0]
    heads = up_key.shape[1] // NOPE
    scale = (NOPE + ROPE) ** (-0.5)
    factor = jnp.exp2(scale_exp.astype(jnp.float32))[:, None]
    q_nope = (query_nope.astype(jnp.float32) * factor).astype(jnp.bfloat16).reshape(queries, heads, NOPE)
    q_rope = (query_rope.astype(jnp.float32) * factor).astype(jnp.bfloat16).reshape(queries, heads, ROPE)
    w_key = up_key.reshape(LATENT, heads, NOPE)
    w_value = up_value.reshape(LATENT, heads, NOPE)
    absorbed = jnp.einsum("qhd,chd->hqc", q_nope, w_key, preferred_element_type=jnp.float32).astype(jnp.bfloat16)
    extended = jnp.concatenate([absorbed, jnp.transpose(q_rope, (1, 0, 2))], axis=2)
    back = jnp.einsum("qhd,chd->hqc", grad_out.reshape(queries, heads, NOPE), w_value,
                      preferred_element_type=jnp.float32).astype(jnp.bfloat16)
    positions = (offsets[:, None] + jnp.arange(QBLOCK, dtype=jnp.int32)[None, :]).reshape(-1)
    latent = whole[:, :LATENT]
    visible = jnp.arange(keys_total, dtype=jnp.int32)[None, :] <= jnp.tile(positions, heads)[:, None]
    along_rows = (((0,), (0,)), ((), ()))
    along_cols = (((1,), (1,)), ((), ()))
    ext_rows = extended.reshape(heads * queries, WIDTH)
    back_rows = back.reshape(heads * queries, LATENT)
    raw = lax.dot_general(ext_rows, whole, along_cols, preferred_element_type=jnp.float32) * scale
    scores = jnp.where(visible, raw, -jnp.inf)
    top = jnp.max(scores, axis=1, keepdims=True)
    lse = top + jnp.log(jnp.sum(jnp.exp(scores - top), axis=1, keepdims=True))
    probs = jnp.exp(scores - lse)
    probs_b = probs.astype(jnp.bfloat16)
    dprob = lax.dot_general(back_rows, latent, along_cols, preferred_element_type=jnp.float32)
    delta = jnp.sum(probs_b.astype(jnp.float32) * dprob, axis=1, keepdims=True)
    dscore = (probs * (dprob - delta) * scale).astype(jnp.bfloat16)
    d_cache = lax.dot_general(dscore, ext_rows, along_rows, preferred_element_type=jnp.float32)
    d_cache = d_cache.at[:, :LATENT].add(
        lax.dot_general(probs_b, back_rows, along_rows, preferred_element_type=jnp.float32))
    split = d_cache.astype(jnp.bfloat16).reshape(16, 4, 2, ROWS, WIDTH)
    split = pack_all(jnp.transpose(split, (2, 1, 0, 3, 4)))
    keep = jnp.where(core == 0, split[0], split[1])
    send = jnp.where(core == 0, split[1], split[0])
    mine = owned_rows(keep, send)
    grad_ext = jnp.dot(dscore, whole, preferred_element_type=jnp.float32)
    grad_abs = grad_ext[:, :LATENT].astype(jnp.bfloat16).reshape(heads, queries, LATENT)
    part_nope = jnp.einsum("hqc,chd->qhd", grad_abs, w_key, preferred_element_type=jnp.float32) * factor[:, :, None]
    part_rope = jnp.transpose(grad_ext[:, LATENT:].reshape(heads, queries, ROPE), (1, 0, 2)) * factor[:, :, None]
    d_query_nope = part_nope.astype(jnp.bfloat16).reshape(queries, heads * NOPE)
    d_query_rope = part_rope.astype(jnp.bfloat16).reshape(queries, heads * ROPE)
    return (mine, d_query_nope, d_query_rope)


def solution(mesh):
    names = SEQ + HEAD
    wide = Mesh(mesh.devices.reshape(8, 2, 4, 2, 2), names)
    in_specs = (
        P(SEQ, None),
        P(SEQ, HEAD),
        P(SEQ, HEAD),
        P(SEQ),
        P(SEQ),
        P(None, HEAD),
        P(None, HEAD),
        P(SEQ, HEAD),
    )
    out_specs = (P(SEQ, None), P(SEQ, HEAD), P(SEQ, HEAD))
    return jax.shard_map(per_device, mesh=wide, in_specs=in_specs, out_specs=out_specs, check_vma=False)
```

```python
import jax
import jax.numpy as jnp
from jax import lax
from jax.experimental import pallas as pl
from jax.experimental.pallas import tpu as pltpu
from jax.sharding import Mesh, PartitionSpec as P

LATENT = 512
ROPE = 64
NOPE = 128
QBLOCK = 64
WIDTH = LATENT + ROPE
LANES = 128
ROWS = 16
PACKED = ROWS * WIDTH // LANES
PADDED = LATENT + LANES
KTILE = 512
VMEM = 56 * 2**20
LOG2E = 1.4426950408889634
UNSEEN = -1e30
SEQ = ("z", "y_lo")
HEAD = ("x", "y_hi", "core")


def pack_rows(rows):
    latent = rows[:, :LATENT].reshape(ROWS, LATENT // LANES, LANES)
    latent = jnp.transpose(latent, (1, 0, 2)).reshape(-1, LANES)
    rotary = rows[:, LATENT:]
    rotary = jnp.concatenate([rotary[: ROWS // 2], rotary[ROWS // 2 :]], axis=1)
    return jnp.concatenate([latent, rotary], axis=0)


def unpack_rows(packed):
    lead = packed.shape[:-2]
    latent = packed[..., : ROWS * LATENT // LANES, :].reshape(*lead, LATENT // LANES, ROWS, LANES)
    latent = jnp.swapaxes(latent, -3, -2).reshape(*lead, ROWS, LATENT)
    rotary = packed[..., ROWS * LATENT // LANES :, :]
    rotary = jnp.concatenate([rotary[..., :ROPE], rotary[..., ROPE:]], axis=-2)
    return jnp.concatenate([latent, rotary], axis=-1)


def to_each(block, axes):
    copies = jnp.broadcast_to(block, (lax.axis_size(axes), *block.shape))
    return lax.all_to_all(copies, axes, 0, 0, tiled=True)


def swap_core(block):
    return lax.ppermute(block, "core", [(0, 1), (1, 0)])


def add_up(blocks):
    return jnp.sum(blocks.astype(jnp.float32), axis=0).astype(jnp.bfloat16)


def owned_rows(keep, send):
    half = (keep.astype(jnp.float32) + swap_core(send).astype(jnp.float32)).astype(jnp.bfloat16)
    slices = add_up(lax.all_to_all(half, "x", 0, 0, tiled=True))
    slices = add_up(lax.all_to_all(slices, SEQ, 0, 0, tiled=True))
    parts = to_each(slices, HEAD)
    sizes = [lax.axis_size(axis) for axis in HEAD]
    parts = parts.reshape(*sizes, PACKED, LANES).astype(jnp.float32)
    parts = jnp.sum(parts, axis=1).astype(jnp.bfloat16)
    return unpack_rows(parts).reshape(-1, WIDTH)


def project_kernel(scale_ref, nope_ref, rope_ref, key_ref, value_ref, grad_ref, ext_ref, back_ref):
    queries = nope_ref.shape[0]
    heads = key_ref.shape[1] // NOPE
    blocks = queries // QBLOCK
    factor = jnp.exp2(scale_ref[...].astype(jnp.float32))
    cols = (((1,), (1,)), ((), ()))
    for h in range(heads):
        lanes = slice(h * NOPE, (h + 1) * NOPE)
        q_nope = (nope_ref[:, lanes].astype(jnp.float32) * factor).astype(jnp.bfloat16)
        absorbed = lax.dot_general(q_nope, key_ref[:, lanes], cols, preferred_element_type=jnp.float32)
        back = lax.dot_general(grad_ref[:, lanes], value_ref[:, lanes], cols, preferred_element_type=jnp.float32)
        absorbed = absorbed.astype(jnp.bfloat16)
        back = back.astype(jnp.bfloat16)
        pair = slice(h // 2 * LANES, (h // 2 + 1) * LANES)
        rope = rope_ref[:, pair].astype(jnp.float32) * factor
        if h % 2:
            rope = pltpu.roll(rope, ROPE, 1)
        lane = lax.broadcasted_iota(jnp.int32, rope.shape, 1)
        rope = jnp.where(lane < ROPE, rope, 0.0).astype(jnp.bfloat16)
        for b in range(blocks):
            src = slice(b * QBLOCK, (b + 1) * QBLOCK)
            dst = slice(h * QBLOCK, (h + 1) * QBLOCK)
            ext_ref[b, dst, :LATENT] = absorbed[src]
            ext_ref[b, dst, LATENT:] = rope[src]
            back_ref[b, dst, :] = back[src]


def project(scale_exp, query_nope, query_rope, up_key, up_value, grad_out):
    queries = query_nope.shape[0]
    heads = up_key.shape[1] // NOPE
    blocks = queries // QBLOCK
    rows = heads * QBLOCK
    return pl.pallas_call(
        project_kernel,
        out_shape=(
            jax.ShapeDtypeStruct((blocks, rows, PADDED), jnp.bfloat16),
            jax.ShapeDtypeStruct((blocks, rows, LATENT), jnp.bfloat16),
        ),
        compiler_params=pltpu.CompilerParams(vmem_limit_bytes=VMEM),
        cost_estimate=pl.CostEstimate(flops=4 * queries * heads * NOPE * LATENT, bytes_accessed=6_000_000, transcendentals=0),
        name="project",
    )(scale_exp.reshape(queries, 1), query_nope, query_rope, up_key, up_value, grad_out)


def attend_kernel(core_ref, offsets_ref, here_ref, there_ref, ext_ref, back_ref,
                  keep_ref, send_ref, ds_ref, cache_ref, score_buf, dprob_buf, acc_buf):
    slices, owners = here_ref.shape[:2]
    keys_total = cache_ref.shape[0]
    blocks, rows = ext_ref.shape[:2]
    core = core_ref[0]
    scale = (NOPE + ROPE) ** (-0.5)
    lane = lax.broadcasted_iota(jnp.int32, (ROWS // 2, LANES), 1)
    span = 2 * slices * ROWS
    lat_rows = ROWS * LATENT // LANES

    def place(s, x, which):
        return pl.multiple_of(s * span + x * 2 * ROWS + which * ROWS, ROWS)

    for s in range(owners):
        for x in range(slices):
            for src, which in ((here_ref, core), (there_ref, 1 - core)):
                row = place(s, x, which)
                for k in range(LATENT // LANES):
                    cache_ref[pl.ds(row, ROWS), k * LANES : (k + 1) * LANES] = src[x, s, k * ROWS : (k + 1) * ROWS, :]
                rope = src[x, s, lat_rows:, :].astype(jnp.float32)
                low = jnp.where(lane < ROPE, rope, 0.0)
                high = jnp.where(lane < ROPE, pltpu.roll(rope, ROPE, 1), 0.0)
                cache_ref[pl.ds(row, ROWS), LATENT:] = jnp.concatenate([low, high], axis=0).astype(jnp.bfloat16)

    cols = (((1,), (1,)), ((), ()))
    tiles = keys_total // KTILE
    inner = lax.broadcasted_iota(jnp.int32, (KTILE, rows), 1) % QBLOCK
    key = lax.broadcasted_iota(jnp.int32, (KTILE, rows), 0)
    ahead = key - inner

    def fold(values, op):
        return op(values.reshape(-1, 8, rows), axis=0)

    def scores(b, t, top):
        keys = slice(t * KTILE, (t + 1) * KTILE)
        raw = lax.dot_general(cache_ref[keys, :], ext_ref[b], cols, preferred_element_type=jnp.float32)
        dprob_buf[b, keys, :] = lax.dot_general(
            cache_ref[keys, :LATENT], back_ref[b], cols, preferred_element_type=jnp.float32)
        raw = jnp.where(ahead <= offsets_ref[b] - t * KTILE, raw * (scale * LOG2E), UNSEEN)
        score_buf[b, keys, :] = raw
        return jnp.maximum(top, fold(raw, jnp.max))

    def weights(b, t, top, total):
        keys = slice(t * KTILE, (t + 1) * KTILE)
        weight = jnp.exp2(score_buf[b, keys, :] - top)
        score_buf[b, keys, :] = weight
        return total + fold(weight, jnp.sum)

    def values(b, t, inverse, delta):
        keys = slice(t * KTILE, (t + 1) * KTILE)
        probs = (score_buf[b, keys, :] * inverse).astype(jnp.bfloat16)
        part = jnp.dot(probs, back_ref[b], preferred_element_type=jnp.float32)
        if b == 0:
            acc_buf[keys, :LATENT] = part
        else:
            acc_buf[keys, :LATENT] += part
        return delta + fold(probs.astype(jnp.float32) * dprob_buf[b, keys, :], jnp.sum)

    def gradients(b, t, inverse, delta):
        keys = slice(t * KTILE, (t + 1) * KTILE)
        dscore = score_buf[b, keys, :] * inverse * (dprob_buf[b, keys, :] - delta) * scale
        dscore = dscore.astype(jnp.bfloat16)
        ds_ref[b, keys, :] = dscore
        part = jnp.dot(dscore, ext_ref[b], preferred_element_type=jnp.float32)
        acc_buf[keys, :LATENT] += part[:, :LATENT]
        if b == 0:
            acc_buf[keys, LATENT:] = part[:, LATENT:]
        else:
            acc_buf[keys, LATENT:] += part[:, LATENT:]

    low = jnp.full((8, rows), UNSEEN, jnp.float32)
    zero = jnp.zeros((8, rows), jnp.float32)
    tops = [low] * blocks
    totals = [zero] * blocks
    deltas = [zero] * blocks
    for t in range(tiles):
        tops[0] = scores(0, t, tops[0])
    tops[0] = jnp.max(tops[0], axis=0, keepdims=True)
    for t in range(tiles):
        tops[1] = scores(1, t, tops[1])
        totals[0] = weights(0, t, tops[0], totals[0])
    tops[1] = jnp.max(tops[1], axis=0, keepdims=True)
    totals[0] = 1.0 / jnp.sum(totals[0], axis=0, keepdims=True)
    for t in range(tiles):
        deltas[0] = values(0, t, totals[0], deltas[0])
        totals[1] = weights(1, t, tops[1], totals[1])
    deltas[0] = jnp.sum(deltas[0], axis=0, keepdims=True)
    totals[1] = 1.0 / jnp.sum(totals[1], axis=0, keepdims=True)
    for t in range(tiles):
        gradients(0, t, totals[0], deltas[0])
        deltas[1] = values(1, t, totals[1], deltas[1])
    deltas[1] = jnp.sum(deltas[1], axis=0, keepdims=True)
    per_tile = KTILE // span
    for t in range(tiles):
        gradients(1, t, totals[1], deltas[1])
        for s in range(t * per_tile, (t + 1) * per_tile):
            for x in range(slices):
                for dst, which in ((send_ref, 1 - core), (keep_ref, core)):
                    row = place(s, x, which)
                    for k in range(LATENT // LANES):
                        dst[x, s, k * ROWS : (k + 1) * ROWS, :] = acc_buf[
                            pl.ds(row, ROWS), k * LANES : (k + 1) * LANES].astype(jnp.bfloat16)
                    rope = acc_buf[pl.ds(row, ROWS), LATENT:]
                    rope = rope[: ROWS // 2] + pltpu.roll(rope[ROWS // 2 :], ROPE, 1)
                    dst[x, s, lat_rows:, :] = rope.astype(jnp.bfloat16)


def attend(core, offsets, here, there, extended, back):
    blocks, rows = extended.shape[:2]
    slices, owners = here.shape[:2]
    keys_total = 2 * slices * owners * ROWS
    packed = jax.ShapeDtypeStruct(here.shape, jnp.bfloat16)
    smem = pl.BlockSpec(memory_space=pltpu.SMEM)
    vmem = pl.BlockSpec(memory_space=pltpu.VMEM)
    return pl.pallas_call(
        attend_kernel,
        out_shape=(
            packed,
            packed,
            jax.ShapeDtypeStruct((blocks, keys_total, rows), jnp.bfloat16),
            jax.ShapeDtypeStruct((keys_total, PADDED), jnp.bfloat16),
        ),
        in_specs=[smem, smem, vmem, vmem, vmem, vmem],
        out_specs=(vmem, vmem, vmem, vmem),
        scratch_shapes=[
            pltpu.VMEM((blocks, keys_total, rows), jnp.float32),
            pltpu.VMEM((blocks, keys_total, rows), jnp.float32),
            pltpu.VMEM((keys_total, PADDED), jnp.float32),
        ],
        compiler_params=pltpu.CompilerParams(vmem_limit_bytes=VMEM),
        cost_estimate=pl.CostEstimate(
            flops=2 * blocks * rows * keys_total * (2 * PADDED + 2 * LATENT),
            bytes_accessed=12_000_000, transcendentals=blocks * rows * keys_total),
        name="attend",
    )(core.reshape(1), offsets, here, there, extended, back)


def query_kernel(scale_ref, ds_ref, cache_ref, key_ref, nope_ref, rope_ref, grad_buf):
    blocks, _, rows = ds_ref.shape
    heads = rows // QBLOCK
    firsts = (((0,), (0,)), ((), ()))
    factor = jnp.exp2(scale_ref[...].astype(jnp.float32))
    for b in range(blocks):
        grad_buf[b] = lax.dot_general(ds_ref[b], cache_ref[...], firsts, preferred_element_type=jnp.float32)
    for h in range(heads):
        lanes = slice(h * NOPE, (h + 1) * NOPE)
        part = slice(h * QBLOCK, (h + 1) * QBLOCK)
        grad = jnp.concatenate([grad_buf[b, part, :] for b in range(blocks)], axis=0)
        nope = jnp.dot(grad[:, :LATENT].astype(jnp.bfloat16), key_ref[:, lanes], preferred_element_type=jnp.float32)
        nope_ref[:, lanes] = (nope * factor).astype(jnp.bfloat16)
        rope = grad[:, LATENT:] * factor
        if h % 2 == 0:
            even = rope
        else:
            pair = slice(h // 2 * LANES, (h // 2 + 1) * LANES)
            rope_ref[:, pair] = (even + pltpu.roll(rope, ROPE, 1)).astype(jnp.bfloat16)


def query_gradients(scale_exp, dscore, cache, up_key):
    blocks, keys_total, rows = dscore.shape
    heads = rows // QBLOCK
    queries = blocks * QBLOCK
    return pl.pallas_call(
        query_kernel,
        out_shape=(
            jax.ShapeDtypeStruct((queries, heads * NOPE), jnp.bfloat16),
            jax.ShapeDtypeStruct((queries, heads * ROPE), jnp.bfloat16),
        ),
        scratch_shapes=[pltpu.VMEM((blocks, rows, PADDED), jnp.float32)],
        compiler_params=pltpu.CompilerParams(vmem_limit_bytes=VMEM),
        cost_estimate=pl.CostEstimate(
            flops=2 * blocks * rows * keys_total * PADDED, bytes_accessed=9_000_000, transcendentals=0),
        name="query_gradients",
    )(scale_exp.reshape(queries, 1), dscore, cache, up_key)


def per_device(cache, query_nope, query_rope, scale_exp, offsets, up_key, up_value, grad_out):
    core = lax.axis_index("core").astype(jnp.int32)
    own = lax.axis_index(("x", "core"))
    mine = pack_rows(lax.dynamic_slice_in_dim(cache, own * ROWS, ROWS, 0))
    over_seq = to_each(mine, SEQ)
    extended, back = project(scale_exp, query_nope, query_rope, up_key, up_value, grad_out)
    over_seq, extended, back = lax.optimization_barrier((over_seq, extended, back))
    here = to_each(over_seq, "x")
    there = swap_core(here)
    keep, send, dscore, whole = attend(core, offsets, here, there, extended, back)
    d_cache = owned_rows(keep, send)
    d_query_nope, d_query_rope = query_gradients(scale_exp, dscore, whole, up_key)
    return (d_cache, d_query_nope, d_query_rope)


def solution(mesh):
    names = SEQ + HEAD
    wide = Mesh(mesh.devices.reshape(8, 2, 4, 2, 2), names)
    in_specs = (
        P(SEQ, None),
        P(SEQ, HEAD),
        P(SEQ, HEAD),
        P(SEQ),
        P(SEQ),
        P(None, HEAD),
        P(None, HEAD),
        P(SEQ, HEAD),
    )
    out_specs = (P(SEQ, None), P(SEQ, HEAD), P(SEQ, HEAD))
    return jax.shard_map(per_device, mesh=wide, in_specs=in_specs, out_specs=out_specs, check_vma=False)
```

```python
import functools

import jax
import jax.numpy as jnp
from jax import lax
from jax.experimental import pallas as pl
from jax.experimental.pallas import tpu as pltpu
from jax.sharding import Mesh, PartitionSpec as P

LATENT = 512
ROPE = 64
NOPE = 128
QBLOCK = 64
WIDTH = LATENT + ROPE
LANES = 128
PADDED = LATENT + LANES
KTILE = 512
GROUPS = 2
VMEM = 44 * 2**20
LOG2E = 1.4426950408889634
UNSEEN = -1e30
SEQ = ("z", "y_lo")
HEAD = ("x", "y_hi", "core")
COLS = (((1,), (1,)), ((), ()))


def to_each(block, axes):
    copies = jnp.broadcast_to(block, (lax.axis_size(axes), *block.shape))
    return lax.all_to_all(copies, axes, 0, 0, tiled=True)


def swap_core(block):
    return lax.ppermute(block, "core", [(0, 1), (1, 0)])


def add_up(blocks):
    return jnp.sum(blocks.astype(jnp.float32), axis=0).astype(jnp.bfloat16)


def owned_columns(keep, send):
    half = (keep.astype(jnp.float32) + swap_core(send).astype(jnp.float32)).astype(jnp.bfloat16)
    slices = add_up(lax.all_to_all(half, "x", 0, 0, tiled=True))
    slices = add_up(lax.all_to_all(slices, SEQ, 0, 0, tiled=True))
    parts = to_each(slices, HEAD)
    sizes = [lax.axis_size(axis) for axis in HEAD]
    parts = parts.reshape(*sizes, *slices.shape).astype(jnp.float32)
    parts = jnp.sum(parts, axis=1).astype(jnp.bfloat16)
    return parts.reshape(-1, slices.shape[-1]).T


def project_kernel(scale_ref, nope_ref, rope_ref, key_ref, value_ref, grad_ref, ext_ref, back_ref, ext_t_ref, back_t_ref):
    queries = nope_ref.shape[0]
    heads = key_ref.shape[1] // NOPE
    factor = jnp.exp2(scale_ref[...].astype(jnp.float32))
    dot = functools.partial(lax.dot_general, dimension_numbers=COLS, preferred_element_type=jnp.float32)
    lane = lax.broadcasted_iota(jnp.int32, (queries, LANES), 1)
    for h in range(heads):
        lanes = slice(h * NOPE, (h + 1) * NOPE)
        rows = slice(h * queries, (h + 1) * queries)
        q_nope = (nope_ref[:, lanes].astype(jnp.float32) * factor).astype(jnp.bfloat16)
        ext_ref[rows, :LATENT] = dot(q_nope, key_ref[:, lanes]).astype(jnp.bfloat16)
        ext_t_ref[:LATENT, rows] = dot(key_ref[:, lanes], q_nope).astype(jnp.bfloat16)
        back_ref[rows, :] = dot(grad_ref[:, lanes], value_ref[:, lanes]).astype(jnp.bfloat16)
        back_t_ref[:, rows] = dot(value_ref[:, lanes], grad_ref[:, lanes]).astype(jnp.bfloat16)
        pair = slice(h // 2 * LANES, (h // 2 + 1) * LANES)
        rope = rope_ref[:, pair].astype(jnp.float32) * factor
        if h % 2:
            rope = pltpu.roll(rope, ROPE, 1)
        rope = jnp.where(lane < ROPE, rope, 0.0)
        ext_ref[rows, LATENT:] = rope.astype(jnp.bfloat16)
        ext_t_ref[LATENT:, rows] = rope.T[:ROPE].astype(jnp.bfloat16)


def project(scale_exp, query_nope, query_rope, up_key, up_value, grad_out):
    queries = query_nope.shape[0]
    heads = up_key.shape[1] // NOPE
    rows = heads * queries
    return pl.pallas_call(
        project_kernel,
        out_shape=(
            jax.ShapeDtypeStruct((rows, PADDED), jnp.bfloat16),
            jax.ShapeDtypeStruct((rows, LATENT), jnp.bfloat16),
            jax.ShapeDtypeStruct((WIDTH, rows), jnp.bfloat16),
            jax.ShapeDtypeStruct((LATENT, rows), jnp.bfloat16),
        ),
        compiler_params=pltpu.CompilerParams(vmem_limit_bytes=24 * 2**20),
        cost_estimate=pl.CostEstimate(flops=8 * rows * NOPE * LATENT, bytes_accessed=7_500_000, transcendentals=0),
        name="project",
    )(scale_exp.reshape(queries, 1), query_nope, query_rope, up_key, up_value, grad_out)


def lay_out(cache_buf, here, there, core):
    slices, owners, height = here.shape[:3]
    for x in range(slices):
        for s in range(owners):
            mine, other = here[x, s], there[x, s]
            first = jnp.where(core == 0, mine, other)
            second = jnp.where(core == 0, other, mine)
            both = jnp.concatenate([first, second], axis=0)
            cache_buf[2 * height * x : 2 * height * (x + 1), s * LANES : (s + 1) * LANES] = both


def attend_kernel(core_ref, offsets_ref, here_hbm, there_hbm, ext_hbm, back_hbm, ext_t_hbm, back_t_hbm,
                  keep_hbm, send_hbm, ds_hbm,
                  here, there, ext, back, ext_t, back_t, cache, bias, score, dprob, acc, ds, keep, send,
                  in_sems, ds_sems, keep_sems, send_sems):
    slices, owners, height = here.shape[:3]
    keys_total = cache.shape[1]
    rows_total = ext.shape[0]
    core = core_ref[0]
    scale = (NOPE + ROPE) ** (-0.5)
    loads = [
        pltpu.make_async_copy(src, dst, in_sems.at[i])
        for i, (src, dst) in enumerate(
            ((here_hbm, here), (there_hbm, there), (ext_hbm, ext), (back_hbm, back), (back_t_hbm, back_t), (ext_t_hbm, ext_t)))
    ]
    for load in loads:
        load.start()

    queries = bias.shape[0]
    row = lax.broadcasted_iota(jnp.int32, (queries, keys_total), 0)
    key = lax.broadcasted_iota(jnp.int32, (queries, keys_total), 1)
    last = row % QBLOCK + jnp.where(row < QBLOCK, offsets_ref[0], offsets_ref[1])
    bias[...] = jnp.where(key <= last, 0.0, UNSEEN)
    cache[WIDTH:, :] = jnp.zeros((PADDED - WIDTH, keys_total), jnp.bfloat16)
    loads[0].wait()
    loads[1].wait()
    lay_out(cache, here, there, core)
    loads[2].wait()
    loads[3].wait()

    tiles = keys_total // KTILE
    rows = rows_total // GROUPS

    def fold(values, op):
        parts = [values[:, k : k + LANES] for k in range(0, KTILE, LANES)]
        return functools.reduce(op, parts)

    def span(g, t):
        return slice(g * rows, (g + 1) * rows), slice(t * KTILE, (t + 1) * KTILE)

    tops = [jnp.full((rows, LANES), UNSEEN, jnp.float32)] * GROUPS
    totals = [jnp.zeros((rows, LANES), jnp.float32)] * GROUPS
    deltas = [jnp.zeros((rows, LANES), jnp.float32)] * GROUPS

    def scores(g, t):
        own, keys = span(g, t)
        raw = jnp.dot(ext[own, :], cache[:, keys], preferred_element_type=jnp.float32)
        seen = jnp.concatenate([bias[:, keys]] * (rows // queries), axis=0)
        raw = raw * (scale * LOG2E) + seen
        score[own, keys] = raw
        tops[g] = jnp.maximum(tops[g], fold(raw, jnp.maximum))
        dprob[own, keys] = jnp.dot(back[own, :], cache[:LATENT, keys], preferred_element_type=jnp.float32)
        if t == tiles - 1:
            tops[g] = jnp.max(tops[g], axis=1, keepdims=True)

    def weights(g, t):
        own, keys = span(g, t)
        weight = jnp.exp2(score[own, keys] - tops[g])
        score[own, keys] = weight
        totals[g] = totals[g] + fold(weight, jnp.add)
        if t == tiles - 1:
            totals[g] = 1.0 / jnp.sum(totals[g], axis=1, keepdims=True)

    def values(g, t):
        own, keys = span(g, t)
        probs = (score[own, keys] * totals[g]).astype(jnp.bfloat16)
        part = jnp.dot(back_t[:, own], probs, preferred_element_type=jnp.float32)
        if g == 0:
            acc[:LATENT, keys] = part
        else:
            acc[:LATENT, keys] += part
        deltas[g] = deltas[g] + fold(probs.astype(jnp.float32) * dprob[own, keys], jnp.add)
        if t == tiles - 1:
            deltas[g] = jnp.sum(deltas[g], axis=1, keepdims=True)

    stores = []

    def gradients(g, t):
        own, keys = span(g, t)
        dscore = score[own, keys] * (totals[g] * scale) * (dprob[own, keys] - deltas[g])
        dscore = dscore.astype(jnp.bfloat16)
        ds[own, keys] = dscore
        store = pltpu.make_async_copy(ds.at[own, keys], ds_hbm.at[own, keys], ds_sems.at[g, t])
        store.start()
        stores.append(store)
        part = jnp.dot(ext_t[:, own], dscore, preferred_element_type=jnp.float32)
        acc[:LATENT, keys] += part[:LATENT]
        if g == 0:
            acc[LATENT:, keys] = part[LATENT:]
        else:
            acc[LATENT:, keys] += part[LATENT:]

    def put_out(t):
        per_tile = KTILE // LANES
        mine = slice(t * per_tile, (t + 1) * per_tile)
        for dst, hbm, sems, which in ((send, send_hbm, send_sems, 1 - core), (keep, keep_hbm, keep_sems, core)):
            for x in range(slices):
                start = pl.multiple_of((2 * x + which) * height, 8)
                for s in range(t * per_tile, (t + 1) * per_tile):
                    dst[x, s] = acc[pl.ds(start, height), s * LANES : (s + 1) * LANES].astype(jnp.bfloat16)
            store = pltpu.make_async_copy(dst.at[:, mine], hbm.at[:, mine], sems.at[t])
            store.start()
            stores.append(store)

    stages = (scores, weights, values, gradients)
    for step in range(len(stages) + GROUPS - 1):
        if step == 2:
            loads[4].wait()
            loads[5].wait()
        for t in range(tiles):
            for g in range(GROUPS):
                if 0 <= step - g < len(stages):
                    stages[step - g](g, t)
            if step == len(stages) + GROUPS - 2:
                put_out(t)
    for store in stores:
        store.wait()


def attend(core, offsets, here, there, ext, back, ext_t, back_t):
    rows = ext.shape[0]
    slices, owners = here.shape[:2]
    keys_total = owners * LANES
    queries = offsets.shape[0] * QBLOCK
    tiles = keys_total // KTILE
    smem = pl.BlockSpec(memory_space=pltpu.SMEM)
    place = pl.BlockSpec(memory_space=pl.ANY)
    bf16, f32 = jnp.bfloat16, jnp.float32
    return pl.pallas_call(
        attend_kernel,
        out_shape=(
            jax.ShapeDtypeStruct(here.shape, bf16),
            jax.ShapeDtypeStruct(here.shape, bf16),
            jax.ShapeDtypeStruct((rows, keys_total), bf16),
        ),
        in_specs=[smem, smem] + [place] * 6,
        out_specs=(place, place, place),
        scratch_shapes=[
            pltpu.VMEM(here.shape, bf16),
            pltpu.VMEM(here.shape, bf16),
            pltpu.VMEM(ext.shape, bf16),
            pltpu.VMEM(back.shape, bf16),
            pltpu.VMEM(ext_t.shape, bf16),
            pltpu.VMEM(back_t.shape, bf16),
            pltpu.VMEM((PADDED, keys_total), bf16),
            pltpu.VMEM((queries, keys_total), f32),
            pltpu.VMEM((rows, keys_total), f32),
            pltpu.VMEM((rows, keys_total), f32),
            pltpu.VMEM((WIDTH, keys_total), f32),
            pltpu.VMEM((rows, keys_total), bf16),
            pltpu.VMEM(here.shape, bf16),
            pltpu.VMEM(here.shape, bf16),
            pltpu.SemaphoreType.DMA((6,)),
            pltpu.SemaphoreType.DMA((GROUPS, tiles)),
            pltpu.SemaphoreType.DMA((tiles,)),
            pltpu.SemaphoreType.DMA((tiles,)),
        ],
        compiler_params=pltpu.CompilerParams(vmem_limit_bytes=VMEM),
        cost_estimate=pl.CostEstimate(
            flops=2 * rows * keys_total * (2 * PADDED + 2 * LATENT),
            bytes_accessed=14_000_000, transcendentals=rows * keys_total),
        name="attend",
    )(core.reshape(1), offsets, here, there, ext, back, ext_t, back_t)


def query_kernel(core_ref, scale_ref, ds_ref, here_ref, there_ref, key_ref, nope_ref, rope_ref, cache, grad_buf):
    queries = nope_ref.shape[0]
    heads = key_ref.shape[1] // NOPE
    factor = jnp.exp2(scale_ref[...].astype(jnp.float32))
    lay_out(cache, here_ref, there_ref, core_ref[0])
    cache[WIDTH:, :] = jnp.zeros((PADDED - WIDTH, cache.shape[1]), jnp.bfloat16)
    grad_buf[...] = lax.dot_general(ds_ref[...], cache[...], COLS, preferred_element_type=jnp.float32)
    for h in range(heads):
        lanes = slice(h * NOPE, (h + 1) * NOPE)
        grad = grad_buf[h * queries : (h + 1) * queries, :]
        nope = jnp.dot(grad[:, :LATENT].astype(jnp.bfloat16), key_ref[:, lanes], preferred_element_type=jnp.float32)
        nope_ref[:, lanes] = (nope * factor).astype(jnp.bfloat16)
        rope = grad[:, LATENT:] * factor
        if h % 2 == 0:
            even = rope
        else:
            pair = slice(h // 2 * LANES, (h // 2 + 1) * LANES)
            rope_ref[:, pair] = (even + pltpu.roll(rope, ROPE, 1)).astype(jnp.bfloat16)


def query_gradients(core, scale_exp, dscore, here, there, up_key):
    rows, keys_total = dscore.shape
    heads = up_key.shape[1] // NOPE
    queries = rows // heads
    smem = pl.BlockSpec(memory_space=pltpu.SMEM)
    vmem = pl.BlockSpec(memory_space=pltpu.VMEM)
    return pl.pallas_call(
        query_kernel,
        out_shape=(
            jax.ShapeDtypeStruct((queries, heads * NOPE), jnp.bfloat16),
            jax.ShapeDtypeStruct((queries, heads * ROPE), jnp.bfloat16),
        ),
        in_specs=[smem] + [vmem] * 5,
        scratch_shapes=[pltpu.VMEM((PADDED, keys_total), jnp.bfloat16), pltpu.VMEM((rows, PADDED), jnp.float32)],
        compiler_params=pltpu.CompilerParams(vmem_limit_bytes=32 * 2**20),
        cost_estimate=pl.CostEstimate(
            flops=2 * rows * keys_total * PADDED, bytes_accessed=9_000_000, transcendentals=0),
        name="query_gradients",
    )(core.reshape(1), scale_exp.reshape(queries, 1), dscore, here, there, up_key)


def per_device(cache, query_nope, query_rope, scale_exp, offsets, up_key, up_value, grad_out):
    core = lax.axis_index("core").astype(jnp.int32)
    own = lax.axis_index(("x", "core"))
    height = WIDTH // (lax.axis_size("x") * lax.axis_size("core"))
    mine = lax.dynamic_slice_in_dim(cache.T, own * height, height, 0)
    over_seq = to_each(mine, SEQ)
    projected = project(scale_exp, query_nope, query_rope, up_key, up_value, grad_out)
    over_seq, projected = lax.optimization_barrier((over_seq, projected))
    here = to_each(over_seq, "x")
    there = swap_core(here)
    keep, send, dscore = attend(core, offsets, here, there, *projected)
    d_cache = owned_columns(keep, send)
    d_query_nope, d_query_rope = query_gradients(core, scale_exp, dscore, here, there, up_key)
    return (d_cache, d_query_nope, d_query_rope)


def solution(mesh):
    wide = Mesh(mesh.devices.reshape(8, 2, 4, 2, 2), SEQ + HEAD)
    in_specs = (
        P(SEQ, None),
        P(SEQ, HEAD),
        P(SEQ, HEAD),
        P(SEQ),
        P(SEQ),
        P(None, HEAD),
        P(None, HEAD),
        P(SEQ, HEAD),
    )
    out_specs = (P(SEQ, None), P(SEQ, HEAD), P(SEQ, HEAD))
    return jax.shard_map(per_device, mesh=wide, in_specs=in_specs, out_specs=out_specs, check_vma=False)
```

```python
import functools

import jax
import jax.numpy as jnp
from jax import lax
from jax.experimental import pallas as pl
from jax.experimental.pallas import tpu as pltpu
from jax.sharding import Mesh, PartitionSpec as P

LATENT = 512
ROPE = 64
NOPE = 128
QBLOCK = 64
WIDTH = LATENT + ROPE
LANES = 128
PADDED = LATENT + LANES
KTILE = 1024
GROUPS = 1
VMEM = 44 * 2**20
LOG2E = 1.4426950408889634
UNSEEN = -1e30
SEQ = ("z", "y_lo")
HEAD = ("x", "y_hi", "core")
COLS = (((1,), (1,)), ((), ()))


def to_each(block, axes):
    copies = jnp.broadcast_to(block, (lax.axis_size(axes), *block.shape))
    return lax.all_to_all(copies, axes, 0, 0, tiled=True)


def swap_core(block):
    return lax.ppermute(block, "core", [(0, 1), (1, 0)])


def add_up(blocks):
    return jnp.sum(blocks.astype(jnp.float32), axis=0).astype(jnp.bfloat16)


def to_next(block):
    size = lax.axis_size("x")
    return lax.ppermute(block, "x", [(i, (i + 1) % size) for i in range(size)])


def to_previous(block):
    size = lax.axis_size("x")
    return lax.ppermute(block, "x", [(i, (i - 1) % size) for i in range(size)])


def gather_over_x(block):
    half = block.shape[0] // 2
    low, high = block[:half], block[half:]
    after_low, before_high = to_previous(low), to_next(high)
    after_high, before_low = to_previous(high), to_next(low)
    far_low, far_high = to_previous(after_low), to_next(before_high)
    return [low, high, after_low, after_high, far_low, far_high, before_low, before_high]


def reduce_over_x(own, after, far, before):
    def send(shift, block):
        return shift(block.astype(jnp.bfloat16)).astype(jnp.float32)

    low = send(to_next, far[0])
    high = send(to_previous, far[1])
    from_before_high = send(to_next, after[1])
    from_after_low = send(to_previous, before[0])
    from_before_low = send(to_next, after[0] + low)
    from_after_high = send(to_previous, before[1] + high)
    return [
        (own[0] + from_before_low + from_after_low).astype(jnp.bfloat16),
        (own[1] + from_before_high + from_after_high).astype(jnp.bfloat16),
    ]


def core_sums(keeps, sends):
    half = keeps[0].shape[0] // 2
    sums = [None] * 4
    for i in (2, 1, 3, 0):
        other = swap_core(sends[i])
        sums[i] = [
            keeps[i][part].astype(jnp.float32) + other[part].astype(jnp.float32)
            for part in (slice(0, half), slice(half, None))
        ]
    return sums


def owned_columns(slices):
    parts = to_each(slices, HEAD)
    sizes = [lax.axis_size(axis) for axis in HEAD]
    parts = parts.reshape(*sizes, *slices.shape).astype(jnp.float32)
    parts = jnp.sum(parts, axis=1).astype(jnp.bfloat16)
    return parts.reshape(-1, slices.shape[-1]).T


def project_kernel(scale_ref, nope_hbm, rope_hbm, key_hbm, value_hbm, grad_hbm, ext_ref, back_ref, ext_t_ref, back_t_ref,
                   nope, rope_in, up_key, up_value, grad, sems):
    queries = nope.shape[0]
    heads = up_key.shape[1] // NOPE
    loads = [
        pltpu.make_async_copy(src, dst, sems.at[i])
        for i, (src, dst) in enumerate(
            ((nope_hbm, nope), (key_hbm, up_key), (rope_hbm, rope_in), (grad_hbm, grad), (value_hbm, up_value)))
    ]
    for load in loads:
        load.start()
    factor = jnp.exp2(scale_ref[...].astype(jnp.float32))
    dot = functools.partial(lax.dot_general, dimension_numbers=COLS, preferred_element_type=jnp.float32)
    lane = lax.broadcasted_iota(jnp.int32, (queries, LANES), 1)
    for load in loads[:3]:
        load.wait()
    for h in range(heads):
        lanes = slice(h * NOPE, (h + 1) * NOPE)
        rows = slice(h * queries, (h + 1) * queries)
        q_nope = (nope[:, lanes].astype(jnp.float32) * factor).astype(jnp.bfloat16)
        ext_ref[rows, :LATENT] = dot(q_nope, up_key[:, lanes]).astype(jnp.bfloat16)
        ext_t_ref[:LATENT, rows] = dot(up_key[:, lanes], q_nope).astype(jnp.bfloat16)
        pair = slice(h // 2 * LANES, (h // 2 + 1) * LANES)
        rope = rope_in[:, pair].astype(jnp.float32) * factor
        if h % 2:
            rope = pltpu.roll(rope, ROPE, 1)
        rope = jnp.where(lane < ROPE, rope, 0.0)
        ext_ref[rows, LATENT:] = rope.astype(jnp.bfloat16)
        ext_t_ref[LATENT:, rows] = rope.T[:ROPE].astype(jnp.bfloat16)
    for load in loads[3:]:
        load.wait()
    for h in range(heads):
        lanes = slice(h * NOPE, (h + 1) * NOPE)
        rows = slice(h * queries, (h + 1) * queries)
        back_ref[rows, :] = dot(grad[:, lanes], up_value[:, lanes]).astype(jnp.bfloat16)
        back_t_ref[:, rows] = dot(up_value[:, lanes], grad[:, lanes]).astype(jnp.bfloat16)


def project(scales, query_nope, query_rope, up_key, up_value, grad_out):
    queries = query_nope.shape[0]
    heads = up_key.shape[1] // NOPE
    rows = heads * queries
    vmem = pl.BlockSpec(memory_space=pltpu.VMEM)
    any_place = pl.BlockSpec(memory_space=pl.ANY)
    operands = (query_nope, query_rope, up_key, up_value, grad_out)
    return pl.pallas_call(
        project_kernel,
        out_shape=(
            jax.ShapeDtypeStruct((rows, PADDED), jnp.bfloat16),
            jax.ShapeDtypeStruct((rows, LATENT), jnp.bfloat16),
            jax.ShapeDtypeStruct((WIDTH, rows), jnp.bfloat16),
            jax.ShapeDtypeStruct((LATENT, rows), jnp.bfloat16),
        ),
        in_specs=[vmem] + [any_place] * len(operands),
        scratch_shapes=[pltpu.VMEM(array.shape, array.dtype) for array in operands]
        + [pltpu.SemaphoreType.DMA((len(operands),))],
        compiler_params=pltpu.CompilerParams(vmem_limit_bytes=58 * 2**20),
        cost_estimate=pl.CostEstimate(flops=8 * rows * NOPE * LATENT, bytes_accessed=7_500_000, transcendentals=0),
        name="project",
    )(scales, *operands)


def fill_cache(cache, blocks, place, core, sems):
    slices = len(blocks) // 4
    half, height = blocks[0].shape[:2]
    copies = []
    for i, block in enumerate(blocks):
        which = core if i < 2 * slices else 1 - core
        x = (place + i % (2 * slices) // 2) % slices
        start = pl.multiple_of((2 * x + which) * height, 8)
        owners = pl.ds(i % 2 * half, half)
        copy = pltpu.make_async_copy(block, cache.at[owners, pl.ds(start, height), :], sems.at[i])
        copy.start()
        copies.append(copy)
    return copies


def keys_of(cache, first, count, features):
    return jnp.concatenate([cache[s, :features, :] for s in range(first, first + count)], axis=1)


def attend_kernel(place_ref, offsets_ref, *refs):
    blocks_hbm, refs = refs[:16], refs[16:]
    (ext_hbm, back_hbm, ext_t_hbm, back_t_hbm), outs_hbm, (ds_hbm, cache_hbm), refs = refs[:4], refs[4:12], refs[12:14], refs[14:]
    (ext, back, ext_t, back_t, cache, bias, score, dprob, acc, ds, outs,
     block_sems, in_sems, ds_sems, out_sems) = refs
    slices = len(outs_hbm) // 2
    height = outs_hbm[0].shape[1]
    place, core = place_ref[0], place_ref[1]
    owners = cache.shape[0]
    keys_total = owners * LANES
    rows_total = ext.shape[0]
    scale = (NOPE + ROPE) ** (-0.5)
    block_loads = fill_cache(cache, blocks_hbm, place, core, block_sems)
    loads = [
        pltpu.make_async_copy(src, dst, in_sems.at[i])
        for i, (src, dst) in enumerate(
            ((ext_hbm, ext), (back_hbm, back), (back_t_hbm, back_t), (ext_t_hbm, ext_t)))
    ]
    loads[0].start()

    queries = bias.shape[0]
    row = lax.broadcasted_iota(jnp.int32, (queries, keys_total), 0)
    key = lax.broadcasted_iota(jnp.int32, (queries, keys_total), 1)
    last = row % QBLOCK + jnp.where(row < QBLOCK, offsets_ref[0], offsets_ref[1])
    bias[...] = jnp.where(key <= last, 0.0, UNSEEN)
    cache[:, WIDTH:, :] = jnp.zeros((owners, PADDED - WIDTH, LANES), jnp.bfloat16)
    for load in block_loads:
        load.wait()
    loads[0].wait()
    for load in loads[1:]:
        load.start()

    tiles = keys_total // KTILE
    per_tile = KTILE // LANES
    rows = rows_total // GROUPS

    def fold(values, op):
        parts = [values[:, k : k + LANES] for k in range(0, KTILE, LANES)]
        return functools.reduce(op, parts)

    def span(g, t):
        return slice(g * rows, (g + 1) * rows), slice(t * KTILE, (t + 1) * KTILE)

    tops = [jnp.full((rows, LANES), UNSEEN, jnp.float32)] * GROUPS
    totals = [jnp.zeros((rows, LANES), jnp.float32)] * GROUPS
    deltas = [jnp.zeros((rows, LANES), jnp.float32)] * GROUPS

    def scores(g, t):
        own, keys = span(g, t)
        mine = keys_of(cache, t * per_tile, per_tile, PADDED)
        raw = jnp.dot(ext[own, :], mine, preferred_element_type=jnp.float32)
        seen = jnp.concatenate([bias[:, keys]] * (rows // queries), axis=0)
        raw = raw * (scale * LOG2E) + seen
        score[own, keys] = raw
        tops[g] = jnp.maximum(tops[g], fold(raw, jnp.maximum))
        if g == 0 and t == 0:
            loads[1].wait()
        dprob[own, keys] = jnp.dot(back[own, :], mine[:LATENT], preferred_element_type=jnp.float32)
        if t == tiles - 1:
            tops[g] = jnp.max(tops[g], axis=1, keepdims=True)

    def weights(g, t):
        own, keys = span(g, t)
        weight = jnp.exp2(score[own, keys] - tops[g])
        score[own, keys] = weight
        totals[g] = totals[g] + fold(weight, jnp.add)
        if t == tiles - 1:
            totals[g] = 1.0 / jnp.sum(totals[g], axis=1, keepdims=True)

    def values(g, t):
        own, keys = span(g, t)
        probs = (score[own, keys] * totals[g]).astype(jnp.bfloat16)
        part = jnp.dot(back_t[:, own], probs, preferred_element_type=jnp.float32)
        if g == 0:
            acc[:LATENT, keys] = part
        else:
            acc[:LATENT, keys] += part
        deltas[g] = deltas[g] + fold(probs.astype(jnp.float32) * dprob[own, keys], jnp.add)
        if t == tiles - 1:
            deltas[g] = jnp.sum(deltas[g], axis=1, keepdims=True)

    stores = [pltpu.make_async_copy(cache, cache_hbm, block_sems.at[len(blocks_hbm)])]
    stores[0].start()

    def gradients(g, t):
        own, keys = span(g, t)
        dscore = score[own, keys] * (totals[g] * scale) * (dprob[own, keys] - deltas[g])
        dscore = dscore.astype(jnp.bfloat16)
        ds[own, keys] = dscore
        store = pltpu.make_async_copy(ds.at[own, keys], ds_hbm.at[own, keys], ds_sems.at[g, t])
        store.start()
        stores.append(store)
        part = jnp.dot(ext_t[:, own], dscore, preferred_element_type=jnp.float32)
        acc[:LATENT, keys] += part[:LATENT]
        if g == 0:
            acc[LATENT:, keys] = part[LATENT:]
        else:
            acc[LATENT:, keys] += part[LATENT:]

    def put_out(t):
        mine = slice(t * per_tile, (t + 1) * per_tile)
        for s in range(t * per_tile, (t + 1) * per_tile):
            outs[s] = acc[:, s * LANES : (s + 1) * LANES].astype(jnp.bfloat16)
        for i, out in enumerate(outs_hbm):
            which = core if i < slices else 1 - core
            start = pl.multiple_of((2 * ((place + i) % slices) + which) * height, 8)
            store = pltpu.make_async_copy(outs.at[mine, pl.ds(start, height), :], out.at[mine], out_sems.at[i, t])
            store.start()
            stores.append(store)

    stages = (scores, weights, values, gradients)
    for step in range(len(stages) + GROUPS - 1):
        if step == stages.index(values):
            loads[2].wait()
            loads[3].wait()
        for t in range(tiles):
            for g in range(GROUPS):
                if 0 <= step - g < len(stages):
                    stages[step - g](g, t)
            if step == len(stages) + GROUPS - 2:
                put_out(t)
    for store in stores:
        store.wait()


def attend(place, offsets, blocks, ext, back, ext_t, back_t):
    rows = ext.shape[0]
    half, height = blocks[0].shape[:2]
    owners = 2 * half
    keys_total = owners * LANES
    queries = offsets.shape[0] * QBLOCK
    tiles = keys_total // KTILE
    smem = pl.BlockSpec(memory_space=pltpu.SMEM)
    any_place = pl.BlockSpec(memory_space=pl.ANY)
    bf16, f32 = jnp.bfloat16, jnp.float32
    sums = len(blocks) // 2
    *outs, dscore, whole = pl.pallas_call(
        attend_kernel,
        out_shape=[jax.ShapeDtypeStruct((owners, height, LANES), bf16)] * sums
        + [jax.ShapeDtypeStruct((rows, keys_total), bf16), jax.ShapeDtypeStruct((owners, PADDED, LANES), bf16)],
        in_specs=[smem, smem] + [any_place] * (len(blocks) + 4),
        out_specs=[any_place] * (sums + 2),
        scratch_shapes=[
            pltpu.VMEM(ext.shape, bf16),
            pltpu.VMEM(back.shape, bf16),
            pltpu.VMEM(ext_t.shape, bf16),
            pltpu.VMEM(back_t.shape, bf16),
            pltpu.VMEM((owners, PADDED, LANES), bf16),
            pltpu.VMEM((queries, keys_total), f32),
            pltpu.VMEM((rows, keys_total), f32),
            pltpu.VMEM((rows, keys_total), f32),
            pltpu.VMEM((WIDTH, keys_total), f32),
            pltpu.VMEM((rows, keys_total), bf16),
            pltpu.VMEM((owners, WIDTH, LANES), bf16),
            pltpu.SemaphoreType.DMA((len(blocks) + 1,)),
            pltpu.SemaphoreType.DMA((4,)),
            pltpu.SemaphoreType.DMA((GROUPS, tiles)),
            pltpu.SemaphoreType.DMA((sums, tiles)),
        ],
        compiler_params=pltpu.CompilerParams(vmem_limit_bytes=VMEM),
        cost_estimate=pl.CostEstimate(
            flops=2 * rows * keys_total * (2 * PADDED + 2 * LATENT),
            bytes_accessed=14_000_000, transcendentals=rows * keys_total),
        name="attend",
    )(place, offsets, *blocks, ext, back, ext_t, back_t)
    return outs[: sums // 2], outs[sums // 2 :], dscore, whole


def query_kernel(first, ready, place_ref, scale_ref, ds_hbm, cache_hbm, key_hbm, *refs):
    nope_hbm, rope_hbm, ds, up_key, parts, cache, grad_buf, nope, rope_out, sems = refs[2 * ready :]
    queries = nope.shape[0]
    heads = up_key.shape[1] // NOPE
    loads = [
        pltpu.make_async_copy(cache_hbm, parts, sems.at[0]),
        pltpu.make_async_copy(ds_hbm.at[first * queries : (first + heads) * queries], ds, sems.at[1]),
        pltpu.make_async_copy(key_hbm.at[:, first * NOPE : (first + heads) * NOPE], up_key, sems.at[2]),
    ]
    for load in loads:
        load.start()
    factor = jnp.exp2(scale_ref[...].astype(jnp.float32))
    loads[0].wait()
    cache[...] = keys_of(parts, 0, parts.shape[0], PADDED)
    loads[1].wait()
    grad_buf[...] = lax.dot_general(ds[...], cache[...], COLS, preferred_element_type=jnp.float32)
    loads[2].wait()
    for h in range(heads):
        lanes = slice(h * NOPE, (h + 1) * NOPE)
        grad = grad_buf[h * queries : (h + 1) * queries, :]
        part = jnp.dot(grad[:, :LATENT].astype(jnp.bfloat16), up_key[:, lanes], preferred_element_type=jnp.float32)
        nope[:, lanes] = (part * factor).astype(jnp.bfloat16)
        rope = grad[:, LATENT:] * factor
        if h % 2 == 0:
            even = rope
        else:
            pair = slice(h // 2 * LANES, (h // 2 + 1) * LANES)
            rope_out[:, pair] = (even + pltpu.roll(rope, ROPE, 1)).astype(jnp.bfloat16)
    stores = [
        pltpu.make_async_copy(nope, nope_hbm.at[:, first * NOPE : (first + heads) * NOPE], sems.at[3]),
        pltpu.make_async_copy(rope_out, rope_hbm.at[:, first * ROPE : (first + heads) * ROPE], sems.at[4]),
    ]
    for store in stores:
        store.start()
    for store in stores:
        store.wait()


def query_gradients(first, count, place, scales, dscore, whole, up_key, ready=()):
    keys_total = dscore.shape[1]
    heads = up_key.shape[1] // NOPE
    queries = scales.shape[0]
    rows = count * queries
    smem = pl.BlockSpec(memory_space=pltpu.SMEM)
    vmem = pl.BlockSpec(memory_space=pltpu.VMEM)
    any_place = pl.BlockSpec(memory_space=pl.ANY)
    bf16, f32 = jnp.bfloat16, jnp.float32
    return pl.pallas_call(
        functools.partial(query_kernel, first, len(ready) // 2),
        out_shape=(
            jax.ShapeDtypeStruct((queries, heads * NOPE), bf16),
            jax.ShapeDtypeStruct((queries, heads * ROPE), bf16),
        ),
        in_specs=[smem, vmem] + [any_place] * (3 + len(ready)),
        out_specs=(any_place, any_place),
        scratch_shapes=[
            pltpu.VMEM((rows, keys_total), bf16),
            pltpu.VMEM((up_key.shape[0], count * NOPE), bf16),
            pltpu.VMEM(whole.shape, bf16),
            pltpu.VMEM((PADDED, keys_total), bf16),
            pltpu.VMEM((rows, PADDED), f32),
            pltpu.VMEM((queries, count * NOPE), bf16),
            pltpu.VMEM((queries, count * ROPE), bf16),
            pltpu.SemaphoreType.DMA((5,)),
        ],
        input_output_aliases={5 + i: i for i in range(len(ready))},
        compiler_params=pltpu.CompilerParams(vmem_limit_bytes=58 * 2**20),
        cost_estimate=pl.CostEstimate(
            flops=2 * rows * keys_total * PADDED, bytes_accessed=9_000_000, transcendentals=0),
        name=f"query_gradients_{first}",
    )(place, scales, dscore, whole, up_key, *ready)


def per_device(cache, query_nope, query_rope, scale_exp, offsets, up_key, up_value, grad_out):
    place = jnp.stack([lax.axis_index("x"), lax.axis_index("core")]).astype(jnp.int32)
    own = lax.axis_index(("x", "core"))
    height = WIDTH // (lax.axis_size("x") * lax.axis_size("core"))
    mine = lax.dynamic_slice_in_dim(cache.T, own * height, height, 0)
    scales = scale_exp.reshape(-1, 1)
    heads = up_key.shape[1] // NOPE
    projected = project(scales, query_nope, query_rope, up_key, up_value, grad_out)
    over_seq, projected = lax.optimization_barrier((to_each(mine, SEQ), projected))
    here = gather_over_x(over_seq)
    blocks = here + [swap_core(block) for block in here]
    keeps, sends, dscore, whole = attend(place, offsets, blocks, *projected)
    slices = jnp.concatenate(reduce_over_x(*core_sums(keeps, sends)))
    early = query_gradients(0, heads // 2, place, scales, dscore, whole, up_key)
    slices = add_up(lax.all_to_all(slices, SEQ, 0, 0, tiled=True))
    slices, early = lax.optimization_barrier((slices, early))
    query_grads = query_gradients(heads // 2, heads // 2, place, scales, dscore, whole, up_key, early)
    return (owned_columns(slices), *query_grads)


def solution(mesh):
    wide = Mesh(mesh.devices.reshape(8, 2, 4, 2, 2), SEQ + HEAD)
    in_specs = (
        P(SEQ, None),
        P(SEQ, HEAD),
        P(SEQ, HEAD),
        P(SEQ),
        P(SEQ),
        P(None, HEAD),
        P(None, HEAD),
        P(SEQ, HEAD),
    )
    out_specs = (P(SEQ, None), P(SEQ, HEAD), P(SEQ, HEAD))
    return jax.shard_map(per_device, mesh=wide, in_specs=in_specs, out_specs=out_specs, check_vma=False)
```

```python
import functools

import jax
import jax.numpy as jnp
from jax import lax
from jax.experimental import pallas as pl
from jax.experimental.pallas import tpu as pltpu
from jax.sharding import Mesh, PartitionSpec as P

LATENT = 512
ROPE = 64
NOPE = 128
QBLOCK = 64
WIDTH = LATENT + ROPE
LANES = 128
PADDED = LATENT + LANES
KTILE = 1024
GROUPS = 1
VMEM = 60 * 2**20
LOG2E = 1.4426950408889634
UNSEEN = -1e30
SEQ = ("z", "y_lo")
HEAD = ("x", "y_hi", "core")
COLS = (((1,), (1,)), ((), ()))


def to_each(block, axes):
    copies = jnp.broadcast_to(block, (lax.axis_size(axes), *block.shape))
    return lax.all_to_all(copies, axes, 0, 0, tiled=True)


def swap_core(block):
    return lax.ppermute(block, "core", [(0, 1), (1, 0)])


def add_up(blocks):
    return jnp.sum(blocks.astype(jnp.float32), axis=0).astype(jnp.bfloat16)


def to_next(block):
    size = lax.axis_size("x")
    return lax.ppermute(block, "x", [(i, (i + 1) % size) for i in range(size)])


def to_previous(block):
    size = lax.axis_size("x")
    return lax.ppermute(block, "x", [(i, (i - 1) % size) for i in range(size)])


def to_side(block):
    size = lax.axis_size("x")
    pairs = [(2 * i + c, 2 * ((i + (1 if c else -1)) % size) + c) for i in range(size) for c in range(2)]
    return lax.ppermute(block, ("x", "core"), pairs)


def to_other_side(block):
    size = lax.axis_size("x")
    pairs = [(2 * i + c, 2 * ((i + (-1 if c else 1)) % size) + c) for i in range(size) for c in range(2)]
    return lax.ppermute(block, ("x", "core"), pairs)


def gather_over_x(block):
    after, before = to_previous(block), to_next(block)
    far = to_side(jnp.where(lax.axis_index("core") == 0, after, before))
    return [block, after, far, before]


def reduce_over_x(own, after, far, before):
    first = lax.axis_index("core") == 0
    passed = to_other_side(far.astype(jnp.bfloat16)).astype(jnp.float32)
    after = to_next((after + jnp.where(first, passed, 0.0)).astype(jnp.bfloat16))
    before = to_previous((before + jnp.where(first, 0.0, passed)).astype(jnp.bfloat16))
    return (own + after.astype(jnp.float32) + before.astype(jnp.float32)).astype(jnp.bfloat16)


def core_sums(keeps, sends):
    sums = [None] * 4
    for i in (2, 1, 3, 0):
        sums[i] = keeps[i].astype(jnp.float32) + swap_core(sends[i]).astype(jnp.float32)
    return sums


def owned_columns(slices):
    parts = to_each(slices, HEAD)
    sizes = [lax.axis_size(axis) for axis in HEAD]
    parts = parts.reshape(*sizes, *slices.shape).astype(jnp.float32)
    parts = jnp.sum(parts, axis=1).astype(jnp.bfloat16)
    return parts.reshape(-1, slices.shape[-1]).T


def project_kernel(scale_ref, nope_hbm, rope_hbm, key_hbm, value_hbm, grad_hbm, ext_ref, back_ref, ext_t_ref, back_t_ref,
                   nope, rope_in, up_key, up_value, grad, sems):
    queries = nope.shape[0]
    heads = up_key.shape[1] // NOPE
    loads = [
        pltpu.make_async_copy(src, dst, sems.at[i])
        for i, (src, dst) in enumerate(
            ((nope_hbm, nope), (key_hbm, up_key), (rope_hbm, rope_in), (grad_hbm, grad), (value_hbm, up_value)))
    ]
    for load in loads:
        load.start()
    factor = jnp.exp2(scale_ref[...].astype(jnp.float32))
    dot = functools.partial(lax.dot_general, dimension_numbers=COLS, preferred_element_type=jnp.float32)
    lane = lax.broadcasted_iota(jnp.int32, (queries, LANES), 1)
    for load in loads[:3]:
        load.wait()
    for h in range(heads):
        lanes = slice(h * NOPE, (h + 1) * NOPE)
        rows = slice(h * queries, (h + 1) * queries)
        q_nope = (nope[:, lanes].astype(jnp.float32) * factor).astype(jnp.bfloat16)
        ext_ref[rows, :LATENT] = dot(q_nope, up_key[:, lanes]).astype(jnp.bfloat16)
        ext_t_ref[:LATENT, rows] = dot(up_key[:, lanes], q_nope).astype(jnp.bfloat16)
        pair = slice(h // 2 * LANES, (h // 2 + 1) * LANES)
        rope = rope_in[:, pair].astype(jnp.float32) * factor
        if h % 2:
            rope = pltpu.roll(rope, ROPE, 1)
        rope = jnp.where(lane < ROPE, rope, 0.0)
        ext_ref[rows, LATENT:] = rope.astype(jnp.bfloat16)
        ext_t_ref[LATENT:, rows] = rope.T[:ROPE].astype(jnp.bfloat16)
    for load in loads[3:]:
        load.wait()
    for h in range(heads):
        lanes = slice(h * NOPE, (h + 1) * NOPE)
        rows = slice(h * queries, (h + 1) * queries)
        back_ref[rows, :] = dot(grad[:, lanes], up_value[:, lanes]).astype(jnp.bfloat16)
        back_t_ref[:, rows] = dot(up_value[:, lanes], grad[:, lanes]).astype(jnp.bfloat16)


def project(scales, query_nope, query_rope, up_key, up_value, grad_out):
    queries = query_nope.shape[0]
    heads = up_key.shape[1] // NOPE
    rows = heads * queries
    vmem = pl.BlockSpec(memory_space=pltpu.VMEM)
    any_place = pl.BlockSpec(memory_space=pl.ANY)
    operands = (query_nope, query_rope, up_key, up_value, grad_out)
    return pl.pallas_call(
        project_kernel,
        out_shape=(
            jax.ShapeDtypeStruct((rows, PADDED), jnp.bfloat16),
            jax.ShapeDtypeStruct((rows, LATENT), jnp.bfloat16),
            jax.ShapeDtypeStruct((WIDTH, rows), jnp.bfloat16),
            jax.ShapeDtypeStruct((LATENT, rows), jnp.bfloat16),
        ),
        in_specs=[vmem] + [any_place] * len(operands),
        scratch_shapes=[pltpu.VMEM(array.shape, array.dtype) for array in operands]
        + [pltpu.SemaphoreType.DMA((len(operands),))],
        compiler_params=pltpu.CompilerParams(vmem_limit_bytes=58 * 2**20),
        cost_estimate=pl.CostEstimate(flops=8 * rows * NOPE * LATENT, bytes_accessed=7_500_000, transcendentals=0),
        name="project",
    )(scales, *operands)


def fill_cache(cache, blocks, place, core, sems):
    slices = len(blocks) // 2
    height = blocks[0].shape[1]
    copies = []
    for i, block in enumerate(blocks):
        which = core if i < slices else 1 - core
        start = pl.multiple_of((2 * ((place + i) % slices) + which) * height, 8)
        copy = pltpu.make_async_copy(block, cache.at[:, pl.ds(start, height), :], sems.at[i])
        copy.start()
        copies.append(copy)
    return copies


def keys_of(cache, first, count, features):
    return jnp.concatenate([cache[s, :features, :] for s in range(first, first + count)], axis=1)


def attend_kernel(place_ref, offsets_ref, *refs):
    blocks_hbm, refs = refs[:8], refs[8:]
    (ext_hbm, back_hbm, ext_t_hbm, back_t_hbm), outs_hbm, (ds_hbm, cache_hbm), refs = refs[:4], refs[4:12], refs[12:14], refs[14:]
    (ext, back, ext_t, back_t, cache, bias, score, dprob, acc, ds, outs,
     block_sems, in_sems, ds_sems, out_sems, cache_sems) = refs
    slices = len(outs_hbm) // 2
    height = outs_hbm[0].shape[1]
    place, core = place_ref[0], place_ref[1]
    owners = cache.shape[0]
    keys_total = owners * LANES
    rows_total = ext.shape[0]
    scale = (NOPE + ROPE) ** (-0.5)
    block_loads = fill_cache(cache, blocks_hbm, place, core, block_sems)
    loads = [
        pltpu.make_async_copy(src, dst, in_sems.at[i])
        for i, (src, dst) in enumerate(
            ((ext_hbm, ext), (back_hbm, back), (back_t_hbm, back_t), (ext_t_hbm, ext_t)))
    ]
    loads[0].start()

    queries = bias.shape[0]
    row = lax.broadcasted_iota(jnp.int32, (queries, keys_total), 0)
    key = lax.broadcasted_iota(jnp.int32, (queries, keys_total), 1)
    last = row % QBLOCK + jnp.where(row < QBLOCK, offsets_ref[0], offsets_ref[1])
    bias[...] = jnp.where(key <= last, 0.0, UNSEEN)
    cache[:, WIDTH:, :] = jnp.zeros((owners, PADDED - WIDTH, LANES), jnp.bfloat16)
    for load in block_loads:
        load.wait()
    loads[0].wait()
    for load in loads[1:]:
        load.start()

    tiles = keys_total // KTILE
    per_tile = KTILE // LANES
    rows = rows_total // GROUPS

    def fold(values, op):
        parts = [values[:, k : k + LANES] for k in range(0, KTILE, LANES)]
        return functools.reduce(op, parts)

    def span(g, t):
        return slice(g * rows, (g + 1) * rows), slice(t * KTILE, (t + 1) * KTILE)

    tops = [jnp.full((rows, LANES), UNSEEN, jnp.float32)] * GROUPS
    totals = [jnp.zeros((rows, LANES), jnp.float32)] * GROUPS
    deltas = [jnp.zeros((rows, LANES), jnp.float32)] * GROUPS

    def scores(g, t):
        own, keys = span(g, t)
        mine = keys_of(cache, t * per_tile, per_tile, PADDED)
        raw = jnp.dot(ext[own, :], mine, preferred_element_type=jnp.float32)
        seen = jnp.concatenate([bias[:, keys]] * (rows // queries), axis=0)
        raw = raw * (scale * LOG2E) + seen
        score[own, keys] = raw
        tops[g] = jnp.maximum(tops[g], fold(raw, jnp.maximum))
        if g == 0 and t == 0:
            loads[1].wait()
        dprob[own, keys] = jnp.dot(back[own, :], mine[:LATENT], preferred_element_type=jnp.float32)
        if t == tiles - 1:
            tops[g] = jnp.max(tops[g], axis=1, keepdims=True)

    def weights(g, t):
        own, keys = span(g, t)
        weight = jnp.exp2(score[own, keys] - tops[g])
        score[own, keys] = weight
        totals[g] = totals[g] + fold(weight, jnp.add)
        if t == tiles - 1:
            totals[g] = 1.0 / jnp.sum(totals[g], axis=1, keepdims=True)

    def values(g, t):
        own, keys = span(g, t)
        probs = (score[own, keys] * totals[g]).astype(jnp.bfloat16)
        part = jnp.dot(back_t[:, own], probs, preferred_element_type=jnp.float32)
        if g == 0:
            acc[:LATENT, keys] = part
        else:
            acc[:LATENT, keys] += part
        deltas[g] = deltas[g] + fold(probs.astype(jnp.float32) * dprob[own, keys], jnp.add)
        if t == tiles - 1:
            deltas[g] = jnp.sum(deltas[g], axis=1, keepdims=True)

    stores = [
        pltpu.make_async_copy(cache.at[s], cache_hbm.at[:, s * LANES : (s + 1) * LANES], cache_sems.at[s])
        for s in range(owners)
    ]
    for store in stores:
        store.start()

    def gradients(g, t):
        own, keys = span(g, t)
        dscore = score[own, keys] * (totals[g] * scale) * (dprob[own, keys] - deltas[g])
        dscore = dscore.astype(jnp.bfloat16)
        ds[own, keys] = dscore
        store = pltpu.make_async_copy(ds.at[own, keys], ds_hbm.at[own, keys], ds_sems.at[g, t])
        store.start()
        stores.append(store)
        part = jnp.dot(ext_t[:, own], dscore, preferred_element_type=jnp.float32)
        acc[:LATENT, keys] += part[:LATENT]
        if g == 0:
            acc[LATENT:, keys] = part[LATENT:]
        else:
            acc[LATENT:, keys] += part[LATENT:]

    def put_out(t):
        mine = slice(t * per_tile, (t + 1) * per_tile)
        for s in range(t * per_tile, (t + 1) * per_tile):
            outs[s] = acc[:, s * LANES : (s + 1) * LANES].astype(jnp.bfloat16)
        for i, out in enumerate(outs_hbm):
            which = core if i < slices else 1 - core
            start = pl.multiple_of((2 * ((place + i) % slices) + which) * height, 8)
            store = pltpu.make_async_copy(outs.at[mine, pl.ds(start, height), :], out.at[mine], out_sems.at[i, t])
            store.start()
            stores.append(store)

    stages = (scores, weights, values, gradients)
    for step in range(len(stages) + GROUPS - 1):
        if step == stages.index(values):
            loads[2].wait()
            loads[3].wait()
        for t in range(tiles):
            for g in range(GROUPS):
                if 0 <= step - g < len(stages):
                    stages[step - g](g, t)
            if step == len(stages) + GROUPS - 2:
                put_out(t)
    for store in stores:
        store.wait()


def attend(place, offsets, blocks, ext, back, ext_t, back_t):
    rows = ext.shape[0]
    owners, height = blocks[0].shape[:2]
    keys_total = owners * LANES
    queries = offsets.shape[0] * QBLOCK
    tiles = keys_total // KTILE
    smem = pl.BlockSpec(memory_space=pltpu.SMEM)
    any_place = pl.BlockSpec(memory_space=pl.ANY)
    bf16, f32 = jnp.bfloat16, jnp.float32
    sums = len(blocks)
    *outs, dscore, whole = pl.pallas_call(
        attend_kernel,
        out_shape=[jax.ShapeDtypeStruct((owners, height, LANES), bf16)] * sums
        + [jax.ShapeDtypeStruct((rows, keys_total), bf16), jax.ShapeDtypeStruct((PADDED, keys_total), bf16)],
        in_specs=[smem, smem] + [any_place] * (len(blocks) + 4),
        out_specs=[any_place] * (sums + 2),
        scratch_shapes=[
            pltpu.VMEM(ext.shape, bf16),
            pltpu.VMEM(back.shape, bf16),
            pltpu.VMEM(ext_t.shape, bf16),
            pltpu.VMEM(back_t.shape, bf16),
            pltpu.VMEM((owners, PADDED, LANES), bf16),
            pltpu.VMEM((queries, keys_total), f32),
            pltpu.VMEM((rows, keys_total), f32),
            pltpu.VMEM((rows, keys_total), f32),
            pltpu.VMEM((WIDTH, keys_total), f32),
            pltpu.VMEM((rows, keys_total), bf16),
            pltpu.VMEM((owners, WIDTH, LANES), bf16),
            pltpu.SemaphoreType.DMA((len(blocks),)),
            pltpu.SemaphoreType.DMA((4,)),
            pltpu.SemaphoreType.DMA((GROUPS, tiles)),
            pltpu.SemaphoreType.DMA((sums, tiles)),
            pltpu.SemaphoreType.DMA((owners,)),
        ],
        compiler_params=pltpu.CompilerParams(vmem_limit_bytes=VMEM),
        cost_estimate=pl.CostEstimate(
            flops=2 * rows * keys_total * (2 * PADDED + 2 * LATENT),
            bytes_accessed=14_000_000, transcendentals=rows * keys_total),
        name="attend",
    )(place, offsets, *blocks, ext, back, ext_t, back_t)
    return outs[: sums // 2], outs[sums // 2 :], dscore, whole


def query_kernel(first, ready, place_ref, scale_ref, ds_hbm, cache_hbm, key_hbm, *refs):
    nope_hbm, rope_hbm, ds, up_key, cache, grad_buf, nope, rope_out, sems = refs[2 * ready :]
    queries = nope.shape[0]
    heads = up_key.shape[1] // NOPE
    loads = [
        pltpu.make_async_copy(cache_hbm, cache, sems.at[0]),
        pltpu.make_async_copy(ds_hbm.at[first * queries : (first + heads) * queries], ds, sems.at[1]),
        pltpu.make_async_copy(key_hbm.at[:, first * NOPE : (first + heads) * NOPE], up_key, sems.at[2]),
    ]
    for load in loads:
        load.start()
    factor = jnp.exp2(scale_ref[...].astype(jnp.float32))
    loads[0].wait()
    loads[1].wait()
    grad_buf[...] = lax.dot_general(ds[...], cache[...], COLS, preferred_element_type=jnp.float32)
    loads[2].wait()
    for h in range(heads):
        lanes = slice(h * NOPE, (h + 1) * NOPE)
        grad = grad_buf[h * queries : (h + 1) * queries, :]
        part = jnp.dot(grad[:, :LATENT].astype(jnp.bfloat16), up_key[:, lanes], preferred_element_type=jnp.float32)
        nope[:, lanes] = (part * factor).astype(jnp.bfloat16)
        rope = grad[:, LATENT:] * factor
        if h % 2 == 0:
            even = rope
        else:
            pair = slice(h // 2 * LANES, (h // 2 + 1) * LANES)
            rope_out[:, pair] = (even + pltpu.roll(rope, ROPE, 1)).astype(jnp.bfloat16)
    stores = [
        pltpu.make_async_copy(nope, nope_hbm.at[:, first * NOPE : (first + heads) * NOPE], sems.at[3]),
        pltpu.make_async_copy(rope_out, rope_hbm.at[:, first * ROPE : (first + heads) * ROPE], sems.at[4]),
    ]
    for store in stores:
        store.start()
    for store in stores:
        store.wait()


def query_gradients(first, count, place, scales, dscore, whole, up_key, ready=()):
    keys_total = dscore.shape[1]
    heads = up_key.shape[1] // NOPE
    queries = scales.shape[0]
    rows = count * queries
    smem = pl.BlockSpec(memory_space=pltpu.SMEM)
    vmem = pl.BlockSpec(memory_space=pltpu.VMEM)
    any_place = pl.BlockSpec(memory_space=pl.ANY)
    bf16, f32 = jnp.bfloat16, jnp.float32
    return pl.pallas_call(
        functools.partial(query_kernel, first, len(ready) // 2),
        out_shape=(
            jax.ShapeDtypeStruct((queries, heads * NOPE), bf16),
            jax.ShapeDtypeStruct((queries, heads * ROPE), bf16),
        ),
        in_specs=[smem, vmem] + [any_place] * (3 + len(ready)),
        out_specs=(any_place, any_place),
        scratch_shapes=[
            pltpu.VMEM((rows, keys_total), bf16),
            pltpu.VMEM((up_key.shape[0], count * NOPE), bf16),
            pltpu.VMEM(whole.shape, bf16),
            pltpu.VMEM((rows, PADDED), f32),
            pltpu.VMEM((queries, count * NOPE), bf16),
            pltpu.VMEM((queries, count * ROPE), bf16),
            pltpu.SemaphoreType.DMA((5,)),
        ],
        input_output_aliases={5 + i: i for i in range(len(ready))},
        compiler_params=pltpu.CompilerParams(vmem_limit_bytes=58 * 2**20),
        cost_estimate=pl.CostEstimate(
            flops=2 * rows * keys_total * PADDED, bytes_accessed=9_000_000, transcendentals=0),
        name=f"query_gradients_{first}",
    )(place, scales, dscore, whole, up_key, *ready)


def per_device(cache, query_nope, query_rope, scale_exp, offsets, up_key, up_value, grad_out):
    place = jnp.stack([lax.axis_index("x"), lax.axis_index("core")]).astype(jnp.int32)
    own = lax.axis_index(("x", "core"))
    height = WIDTH // (lax.axis_size("x") * lax.axis_size("core"))
    mine = lax.dynamic_slice_in_dim(cache.T, own * height, height, 0)
    scales = scale_exp.reshape(-1, 1)
    heads = up_key.shape[1] // NOPE
    projected = project(scales, query_nope, query_rope, up_key, up_value, grad_out)
    over_seq, projected = lax.optimization_barrier((to_each(mine, SEQ), projected))
    here = gather_over_x(over_seq)
    blocks = here + [swap_core(block) for block in here]
    keeps, sends, dscore, whole = attend(place, offsets, blocks, *projected)
    slices = reduce_over_x(*core_sums(keeps, sends))
    early = query_gradients(0, heads // 2, place, scales, dscore, whole, up_key)
    slices, early = lax.optimization_barrier((slices, early))
    query_grads = query_gradients(heads // 2, heads // 2, place, scales, dscore, whole, up_key, early)
    slices = add_up(lax.all_to_all(slices, SEQ, 0, 0, tiled=True))
    slices, query_grads = lax.optimization_barrier((slices, query_grads))
    return (owned_columns(slices), *query_grads)


def solution(mesh):
    wide = Mesh(mesh.devices.reshape(8, 2, 4, 2, 2), SEQ + HEAD)
    in_specs = (
        P(SEQ, None),
        P(SEQ, HEAD),
        P(SEQ, HEAD),
        P(SEQ),
        P(SEQ),
        P(None, HEAD),
        P(None, HEAD),
        P(SEQ, HEAD),
    )
    out_specs = (P(SEQ, None), P(SEQ, HEAD), P(SEQ, HEAD))
    return jax.shard_map(per_device, mesh=wide, in_specs=in_specs, out_specs=out_specs, check_vma=False)
```

```python
import functools

import jax
import jax.numpy as jnp
from jax import lax
from jax.experimental import pallas as pl
from jax.experimental.pallas import tpu as pltpu
from jax.sharding import Mesh, PartitionSpec as P

LATENT = 512
ROPE = 64
NOPE = 128
QBLOCK = 64
WIDTH = LATENT + ROPE
LANES = 128
PADDED = LATENT + LANES
KTILE = 1024
GROUPS = 1
VMEM = 60 * 2**20
LOG2E = 1.4426950408889634
UNSEEN = -1e30
SEQ = ("z", "y_lo")
HEAD = ("x", "y_hi", "core")
COLS = (((1,), (1,)), ((), ()))


def to_each(block, axes):
    copies = jnp.broadcast_to(block, (lax.axis_size(axes), *block.shape))
    return lax.all_to_all(copies, axes, 0, 0, tiled=True)


def swap_core(block):
    return lax.ppermute(block, "core", [(0, 1), (1, 0)])


def add_up(blocks):
    return jnp.sum(blocks.astype(jnp.float32), axis=0).astype(jnp.bfloat16)


def to_next(block):
    size = lax.axis_size("x")
    return lax.ppermute(block, "x", [(i, (i + 1) % size) for i in range(size)])


def to_previous(block):
    size = lax.axis_size("x")
    return lax.ppermute(block, "x", [(i, (i - 1) % size) for i in range(size)])


def to_side(block):
    size = lax.axis_size("x")
    pairs = [(2 * i + c, 2 * ((i + (-1 if c else 1)) % size) + c) for i in range(size) for c in range(2)]
    return lax.ppermute(block, ("x", "core"), pairs)


def gather_over_x(block):
    half = block.shape[0] // 2
    return [block, to_previous(block[:half]), to_next(block[half:])]


def reduce_over_x(own, after, far, before):
    first = lax.axis_index("core") == 0
    passed = to_side(far.astype(jnp.bfloat16)).astype(jnp.float32)
    after = to_next((after + jnp.where(first, passed, 0.0)).astype(jnp.bfloat16))
    before = to_previous((before + jnp.where(first, 0.0, passed)).astype(jnp.bfloat16))
    return (own + after.astype(jnp.float32) + before.astype(jnp.float32)).astype(jnp.bfloat16)


def core_sums(keeps, sends):
    sums = [None] * 4
    for i in (2, 1, 3, 0):
        sums[i] = keeps[i].astype(jnp.float32) + swap_core(sends[i]).astype(jnp.float32)
    return sums


def owned_columns(slices):
    parts = to_each(slices, HEAD)
    sizes = [lax.axis_size(axis) for axis in HEAD]
    parts = parts.reshape(*sizes, *slices.shape).astype(jnp.float32)
    parts = jnp.sum(parts, axis=1).astype(jnp.bfloat16)
    return parts.reshape(-1, slices.shape[-1]).T


def project_kernel(scale_ref, nope_hbm, rope_hbm, key_hbm, value_hbm, grad_hbm, ext_ref, back_ref, ext_t_ref, back_t_ref,
                   nope, rope_in, up_key, up_value, grad, sems):
    queries = nope.shape[0]
    heads = up_key.shape[1] // NOPE
    loads = [
        pltpu.make_async_copy(src, dst, sems.at[i])
        for i, (src, dst) in enumerate(
            ((nope_hbm, nope), (key_hbm, up_key), (rope_hbm, rope_in), (grad_hbm, grad), (value_hbm, up_value)))
    ]
    for load in loads:
        load.start()
    factor = jnp.exp2(scale_ref[...].astype(jnp.float32))
    dot = functools.partial(lax.dot_general, dimension_numbers=COLS, preferred_element_type=jnp.float32)
    lane = lax.broadcasted_iota(jnp.int32, (queries, LANES), 1)
    for load in loads[:3]:
        load.wait()
    for h in range(heads):
        lanes = slice(h * NOPE, (h + 1) * NOPE)
        rows = slice(h * queries, (h + 1) * queries)
        q_nope = (nope[:, lanes].astype(jnp.float32) * factor).astype(jnp.bfloat16)
        ext_ref[rows, :LATENT] = dot(q_nope, up_key[:, lanes]).astype(jnp.bfloat16)
        ext_t_ref[:LATENT, rows] = dot(up_key[:, lanes], q_nope).astype(jnp.bfloat16)
        pair = slice(h // 2 * LANES, (h // 2 + 1) * LANES)
        rope = rope_in[:, pair].astype(jnp.float32) * factor
        if h % 2:
            rope = pltpu.roll(rope, ROPE, 1)
        rope = jnp.where(lane < ROPE, rope, 0.0)
        ext_ref[rows, LATENT:] = rope.astype(jnp.bfloat16)
        ext_t_ref[LATENT:, rows] = rope.T[:ROPE].astype(jnp.bfloat16)
    for load in loads[3:]:
        load.wait()
    for h in range(heads):
        lanes = slice(h * NOPE, (h + 1) * NOPE)
        rows = slice(h * queries, (h + 1) * queries)
        back_ref[rows, :] = dot(grad[:, lanes], up_value[:, lanes]).astype(jnp.bfloat16)
        back_t_ref[:, rows] = dot(up_value[:, lanes], grad[:, lanes]).astype(jnp.bfloat16)


def project(scales, query_nope, query_rope, up_key, up_value, grad_out):
    queries = query_nope.shape[0]
    heads = up_key.shape[1] // NOPE
    rows = heads * queries
    vmem = pl.BlockSpec(memory_space=pltpu.VMEM)
    any_place = pl.BlockSpec(memory_space=pl.ANY)
    operands = (query_nope, query_rope, up_key, up_value, grad_out)
    return pl.pallas_call(
        project_kernel,
        out_shape=(
            jax.ShapeDtypeStruct((rows, PADDED), jnp.bfloat16),
            jax.ShapeDtypeStruct((rows, LATENT), jnp.bfloat16),
            jax.ShapeDtypeStruct((WIDTH, rows), jnp.bfloat16),
            jax.ShapeDtypeStruct((LATENT, rows), jnp.bfloat16),
        ),
        in_specs=[vmem] + [any_place] * len(operands),
        scratch_shapes=[pltpu.VMEM(array.shape, array.dtype) for array in operands]
        + [pltpu.SemaphoreType.DMA((len(operands),))],
        compiler_params=pltpu.CompilerParams(vmem_limit_bytes=58 * 2**20),
        cost_estimate=pl.CostEstimate(flops=8 * rows * NOPE * LATENT, bytes_accessed=7_500_000, transcendentals=0),
        name="project",
    )(scales, *operands)


def fill_cache(cache, blocks, place, core, sems):
    parts = len(blocks) // 2
    half, height = blocks[1].shape[:2]
    copies = []
    for i, block in enumerate(blocks):
        which = core if i < parts else 1 - core
        parity = (place + (i % parts > 0)) % 2
        owners = ((0, 2 * half), (0, half), (half, half))[i % parts]
        start = pl.multiple_of((2 * parity + which) * height, 16)
        copy = pltpu.make_async_copy(block, cache.at[pl.ds(*owners), pl.ds(start, height), :], sems.at[i])
        copy.start()
        copies.append(copy)
    return copies


def keys_of(cache, first, count, features):
    return jnp.concatenate([cache[s, :features, :] for s in range(first, first + count)], axis=1)


def attend_kernel(place_ref, offsets_ref, *refs):
    blocks_hbm, refs = refs[:6], refs[6:]
    (ext_hbm, back_hbm, ext_t_hbm, back_t_hbm), outs_hbm, (ds_hbm, cache_hbm), refs = refs[:4], refs[4:12], refs[12:14], refs[14:]
    (ext, back, ext_t, back_t, cache, bias, score, dprob, acc, ds, outs,
     block_sems, in_sems, ds_sems, out_sems) = refs
    slices = len(outs_hbm) // 2
    height = outs_hbm[0].shape[1]
    place, core = place_ref[0], place_ref[1]
    owners = cache.shape[0]
    keys_total = owners * LANES
    rows_total = ext.shape[0]
    scale = (NOPE + ROPE) ** (-0.5)
    block_loads = fill_cache(cache, blocks_hbm, place, core, block_sems)
    loads = [
        pltpu.make_async_copy(src, dst, in_sems.at[i])
        for i, (src, dst) in enumerate(
            ((ext_hbm, ext), (back_hbm, back), (back_t_hbm, back_t), (ext_t_hbm, ext_t)))
    ]
    loads[0].start()

    queries = bias.shape[0]
    row = lax.broadcasted_iota(jnp.int32, (queries, keys_total), 0)
    key = lax.broadcasted_iota(jnp.int32, (queries, keys_total), 1)
    last = row % QBLOCK + jnp.where(row < QBLOCK, offsets_ref[0], offsets_ref[1])
    bias[...] = jnp.where(key <= last, 0.0, UNSEEN)
    cache[:, WIDTH:, :] = jnp.zeros((owners, PADDED - WIDTH, LANES), jnp.bfloat16)
    for load in block_loads:
        load.wait()
    loads[0].wait()
    for load in loads[1:]:
        load.start()

    tiles = keys_total // KTILE
    per_tile = KTILE // LANES
    rows = rows_total // GROUPS

    def fold(values, op):
        parts = [values[:, k : k + LANES] for k in range(0, KTILE, LANES)]
        return functools.reduce(op, parts)

    def span(g, t):
        return slice(g * rows, (g + 1) * rows), slice(t * KTILE, (t + 1) * KTILE)

    tops = [jnp.full((rows, LANES), UNSEEN, jnp.float32)] * GROUPS
    totals = [jnp.zeros((rows, LANES), jnp.float32)] * GROUPS
    deltas = [jnp.zeros((rows, LANES), jnp.float32)] * GROUPS

    def scores(g, t):
        own, keys = span(g, t)
        mine = keys_of(cache, t * per_tile, per_tile, PADDED)
        raw = jnp.dot(ext[own, :], mine, preferred_element_type=jnp.float32)
        seen = jnp.concatenate([bias[:, keys]] * (rows // queries), axis=0)
        raw = raw * (scale * LOG2E) + seen
        score[own, keys] = raw
        tops[g] = jnp.maximum(tops[g], fold(raw, jnp.maximum))
        if g == 0 and t == 0:
            loads[1].wait()
        dprob[own, keys] = jnp.dot(back[own, :], mine[:LATENT], preferred_element_type=jnp.float32)
        if t == tiles - 1:
            tops[g] = jnp.max(tops[g], axis=1, keepdims=True)

    def weights(g, t):
        own, keys = span(g, t)
        weight = jnp.exp2(score[own, keys] - tops[g])
        score[own, keys] = weight
        totals[g] = totals[g] + fold(weight, jnp.add)
        if t == tiles - 1:
            totals[g] = 1.0 / jnp.sum(totals[g], axis=1, keepdims=True)

    def values(g, t):
        own, keys = span(g, t)
        probs = (score[own, keys] * totals[g]).astype(jnp.bfloat16)
        part = jnp.dot(back_t[:, own], probs, preferred_element_type=jnp.float32)
        if g == 0:
            acc[:LATENT, keys] = part
        else:
            acc[:LATENT, keys] += part
        deltas[g] = deltas[g] + fold(probs.astype(jnp.float32) * dprob[own, keys], jnp.add)
        if t == tiles - 1:
            deltas[g] = jnp.sum(deltas[g], axis=1, keepdims=True)

    stores = [pltpu.make_async_copy(cache, cache_hbm, block_sems.at[len(blocks_hbm)])]
    stores[0].start()

    def gradients(g, t):
        own, keys = span(g, t)
        dscore = score[own, keys] * (totals[g] * scale) * (dprob[own, keys] - deltas[g])
        dscore = dscore.astype(jnp.bfloat16)
        ds[own, keys] = dscore
        store = pltpu.make_async_copy(ds.at[own, keys], ds_hbm.at[own, keys], ds_sems.at[g, t])
        store.start()
        stores.append(store)
        part = jnp.dot(ext_t[:, own], dscore, preferred_element_type=jnp.float32)
        acc[:LATENT, keys] += part[:LATENT]
        if g == 0:
            acc[LATENT:, keys] = part[LATENT:]
        else:
            acc[LATENT:, keys] += part[LATENT:]

    def put_out(t):
        mine = slice(t * per_tile, (t + 1) * per_tile)
        for s in range(t * per_tile, (t + 1) * per_tile):
            outs[s] = acc[:, s * LANES : (s + 1) * LANES].astype(jnp.bfloat16)
        for i, out in enumerate(outs_hbm):
            which = core if i < slices else 1 - core
            start = pl.multiple_of((2 * ((place + i) % slices) + which) * height, 8)
            store = pltpu.make_async_copy(outs.at[mine, pl.ds(start, height), :], out.at[mine], out_sems.at[i, t])
            store.start()
            stores.append(store)

    stages = (scores, weights, values, gradients)
    for step in range(len(stages) + GROUPS - 1):
        if step == stages.index(values):
            loads[2].wait()
            loads[3].wait()
        for t in range(tiles):
            for g in range(GROUPS):
                if 0 <= step - g < len(stages):
                    stages[step - g](g, t)
            if step == len(stages) + GROUPS - 2:
                put_out(t)
    for store in stores:
        store.wait()


def attend(slices, place, offsets, blocks, ext, back, ext_t, back_t):
    rows = ext.shape[0]
    owners = blocks[0].shape[0]
    height = WIDTH // (2 * slices)
    keys_total = owners * LANES
    queries = offsets.shape[0] * QBLOCK
    tiles = keys_total // KTILE
    smem = pl.BlockSpec(memory_space=pltpu.SMEM)
    any_place = pl.BlockSpec(memory_space=pl.ANY)
    bf16, f32 = jnp.bfloat16, jnp.float32
    sums = 2 * slices
    *outs, dscore, whole = pl.pallas_call(
        attend_kernel,
        out_shape=[jax.ShapeDtypeStruct((owners, height, LANES), bf16)] * sums
        + [jax.ShapeDtypeStruct((rows, keys_total), bf16), jax.ShapeDtypeStruct((owners, PADDED, LANES), bf16)],
        in_specs=[smem, smem] + [any_place] * (len(blocks) + 4),
        out_specs=[any_place] * (sums + 2),
        scratch_shapes=[
            pltpu.VMEM(ext.shape, bf16),
            pltpu.VMEM(back.shape, bf16),
            pltpu.VMEM(ext_t.shape, bf16),
            pltpu.VMEM(back_t.shape, bf16),
            pltpu.VMEM((owners, PADDED, LANES), bf16),
            pltpu.VMEM((queries, keys_total), f32),
            pltpu.VMEM((rows, keys_total), f32),
            pltpu.VMEM((rows, keys_total), f32),
            pltpu.VMEM((WIDTH, keys_total), f32),
            pltpu.VMEM((rows, keys_total), bf16),
            pltpu.VMEM((owners, WIDTH, LANES), bf16),
            pltpu.SemaphoreType.DMA((len(blocks) + 1,)),
            pltpu.SemaphoreType.DMA((4,)),
            pltpu.SemaphoreType.DMA((GROUPS, tiles)),
            pltpu.SemaphoreType.DMA((sums, tiles)),
        ],
        compiler_params=pltpu.CompilerParams(vmem_limit_bytes=VMEM),
        cost_estimate=pl.CostEstimate(
            flops=2 * rows * keys_total * (2 * PADDED + 2 * LATENT),
            bytes_accessed=14_000_000, transcendentals=rows * keys_total),
        name="attend",
    )(place, offsets, *blocks, ext, back, ext_t, back_t)
    return outs[: sums // 2], outs[sums // 2 :], dscore, whole


def query_kernel(scale_ref, ds_hbm, cache_hbm, key_hbm, *refs):
    nope_ref, rope_ref, ds, up_key, parts, cache, grad_buf, sems = refs
    queries = nope_ref.shape[0]
    half = ds.shape[0] // 2
    heads = up_key.shape[1] // NOPE
    loads = [
        pltpu.make_async_copy(cache_hbm, parts, sems.at[0]),
        pltpu.make_async_copy(ds_hbm.at[:half], ds.at[:half], sems.at[1]),
        pltpu.make_async_copy(ds_hbm.at[half:], ds.at[half:], sems.at[2]),
        pltpu.make_async_copy(key_hbm, up_key, sems.at[3]),
    ]
    for load in loads:
        load.start()
    factor = jnp.exp2(scale_ref[...].astype(jnp.float32))
    loads[0].wait()
    cache[...] = keys_of(parts, 0, parts.shape[0], PADDED)
    for i in range(2):
        own = slice(i * half, (i + 1) * half)
        loads[1 + i].wait()
        grad_buf[own, :] = lax.dot_general(ds[own, :], cache[...], COLS, preferred_element_type=jnp.float32)
    loads[3].wait()
    for h in range(heads):
        lanes = slice(h * NOPE, (h + 1) * NOPE)
        grad = grad_buf[h * queries : (h + 1) * queries, :]
        part = jnp.dot(grad[:, :LATENT].astype(jnp.bfloat16), up_key[:, lanes], preferred_element_type=jnp.float32)
        nope_ref[:, lanes] = (part * factor).astype(jnp.bfloat16)
        rope = grad[:, LATENT:] * factor
        if h % 2 == 0:
            even = rope
        else:
            pair = slice(h // 2 * LANES, (h // 2 + 1) * LANES)
            rope_ref[:, pair] = (even + pltpu.roll(rope, ROPE, 1)).astype(jnp.bfloat16)


def query_gradients(scales, dscore, whole, up_key):
    rows, keys_total = dscore.shape
    heads = up_key.shape[1] // NOPE
    queries = scales.shape[0]
    vmem = pl.BlockSpec(memory_space=pltpu.VMEM)
    any_place = pl.BlockSpec(memory_space=pl.ANY)
    bf16, f32 = jnp.bfloat16, jnp.float32
    return pl.pallas_call(
        query_kernel,
        out_shape=(
            jax.ShapeDtypeStruct((queries, heads * NOPE), bf16),
            jax.ShapeDtypeStruct((queries, heads * ROPE), bf16),
        ),
        in_specs=[vmem] + [any_place] * 3,
        scratch_shapes=[
            pltpu.VMEM(dscore.shape, bf16),
            pltpu.VMEM(up_key.shape, bf16),
            pltpu.VMEM(whole.shape, bf16),
            pltpu.VMEM((PADDED, keys_total), bf16),
            pltpu.VMEM((rows, PADDED), f32),
            pltpu.SemaphoreType.DMA((4,)),
        ],
        compiler_params=pltpu.CompilerParams(vmem_limit_bytes=58 * 2**20),
        cost_estimate=pl.CostEstimate(
            flops=2 * rows * keys_total * PADDED, bytes_accessed=9_000_000, transcendentals=0),
        name="query_gradients",
    )(scales, dscore, whole, up_key)


def per_device(cache, query_nope, query_rope, scale_exp, offsets, up_key, up_value, grad_out):
    place = jnp.stack([lax.axis_index("x"), lax.axis_index("core")]).astype(jnp.int32)
    own = place[0] % 2 * 2 + place[1]
    height = WIDTH // 4
    mine = lax.dynamic_slice_in_dim(cache.T, own * height, height, 0)
    scales = scale_exp.reshape(-1, 1)
    projected = project(scales, query_nope, query_rope, up_key, up_value, grad_out)
    over_seq, projected = lax.optimization_barrier((to_each(mine, SEQ), projected))
    here = gather_over_x(over_seq)
    blocks = here + [swap_core(block) for block in here]
    keeps, sends, dscore, whole = attend(lax.axis_size("x"), place, offsets, blocks, *projected)
    slices = reduce_over_x(*core_sums(keeps, sends))
    query_grads = query_gradients(scales, dscore, whole, up_key)
    slices = add_up(lax.all_to_all(slices, SEQ, 0, 0, tiled=True))
    slices, query_grads = lax.optimization_barrier((slices, query_grads))
    return (owned_columns(slices), *query_grads)


def solution(mesh):
    wide = Mesh(mesh.devices.reshape(8, 2, 4, 2, 2), SEQ + HEAD)
    in_specs = (
        P(SEQ, None),
        P(SEQ, HEAD),
        P(SEQ, HEAD),
        P(SEQ),
        P(SEQ),
        P(None, HEAD),
        P(None, HEAD),
        P(SEQ, HEAD),
    )
    out_specs = (P(SEQ, None), P(SEQ, HEAD), P(SEQ, HEAD))
    return jax.shard_map(per_device, mesh=wide, in_specs=in_specs, out_specs=out_specs, check_vma=False)
```

```python
import functools

import jax
import jax.numpy as jnp
from jax import lax
from jax.experimental import pallas as pl
from jax.experimental.pallas import tpu as pltpu
from jax.sharding import Mesh, PartitionSpec as P

LATENT = 512
ROPE = 64
NOPE = 128
QBLOCK = 64
WIDTH = LATENT + ROPE
LANES = 128
PADDED = LATENT + LANES
KTILE = 1024
GROUPS = 1
VMEM = 49 * 2**20
LOG2E = 1.4426950408889634
UNSEEN = -1e30
SEQ = ("z", "y_lo")
HEAD = ("x", "y_hi", "core")
COLS = (((1,), (1,)), ((), ()))


def to_each(block, axes):
    copies = jnp.broadcast_to(block, (lax.axis_size(axes), *block.shape))
    return lax.all_to_all(copies, axes, 0, 0, tiled=True)


def swap_core(block):
    return lax.ppermute(block, "core", [(0, 1), (1, 0)])


def add_up(blocks):
    return jnp.sum(blocks.astype(jnp.float32), axis=0).astype(jnp.bfloat16)


def to_next(block):
    size = lax.axis_size("x")
    return lax.ppermute(block, "x", [(i, (i + 1) % size) for i in range(size)])


def to_previous(block):
    size = lax.axis_size("x")
    return lax.ppermute(block, "x", [(i, (i - 1) % size) for i in range(size)])


def to_side(block):
    size = lax.axis_size("x")
    pairs = [(2 * i + c, 2 * ((i + (-1 if c else 1)) % size) + c) for i in range(size) for c in range(2)]
    return lax.ppermute(block, ("x", "core"), pairs)


def gather_over_x(block):
    half = block.shape[0] // 2
    return [block, to_previous(block[:half]), to_next(block[half:])]


def reduce_over_x(own, after, far, before):
    first = lax.axis_index("core") == 0
    passed = to_side(far.astype(jnp.bfloat16)).astype(jnp.float32)
    after = to_next((after + jnp.where(first, passed, 0.0)).astype(jnp.bfloat16))
    before = to_previous((before + jnp.where(first, 0.0, passed)).astype(jnp.bfloat16))
    return (own + after.astype(jnp.float32) + before.astype(jnp.float32)).astype(jnp.bfloat16)


def core_sums(keeps, sends):
    sums = [None] * 4
    for i in (2, 1, 3, 0):
        sums[i] = keeps[i].astype(jnp.float32) + swap_core(sends[i]).astype(jnp.float32)
    return sums


def owned_columns(slices):
    parts = to_each(slices, HEAD)
    sizes = [lax.axis_size(axis) for axis in HEAD]
    parts = parts.reshape(*sizes, *slices.shape).astype(jnp.float32)
    parts = jnp.sum(parts, axis=1).astype(jnp.bfloat16)
    return parts.reshape(-1, slices.shape[-1]).T


def project_kernel(scale_ref, nope_hbm, rope_hbm, key_hbm, value_hbm, grad_hbm, ext_ref, back_ref, ext_t_ref, back_t_ref,
                   nope, rope_in, up_key, up_value, grad, sems):
    queries = nope.shape[0]
    heads = up_key.shape[1] // NOPE
    loads = [
        pltpu.make_async_copy(src, dst, sems.at[i])
        for i, (src, dst) in enumerate(
            ((nope_hbm, nope), (key_hbm, up_key), (rope_hbm, rope_in), (grad_hbm, grad), (value_hbm, up_value)))
    ]
    for load in loads:
        load.start()
    factor = jnp.exp2(scale_ref[...].astype(jnp.float32))
    dot = functools.partial(lax.dot_general, dimension_numbers=COLS, preferred_element_type=jnp.float32)
    lane = lax.broadcasted_iota(jnp.int32, (queries, LANES), 1)
    for load in loads[:3]:
        load.wait()
    for h in range(heads):
        lanes = slice(h * NOPE, (h + 1) * NOPE)
        rows = slice(h * queries, (h + 1) * queries)
        q_nope = (nope[:, lanes].astype(jnp.float32) * factor).astype(jnp.bfloat16)
        ext_ref[rows, :LATENT] = dot(q_nope, up_key[:, lanes]).astype(jnp.bfloat16)
        ext_t_ref[:LATENT, rows] = dot(up_key[:, lanes], q_nope).astype(jnp.bfloat16)
        pair = slice(h // 2 * LANES, (h // 2 + 1) * LANES)
        rope = rope_in[:, pair].astype(jnp.float32) * factor
        if h % 2:
            rope = pltpu.roll(rope, ROPE, 1)
        rope = jnp.where(lane < ROPE, rope, 0.0)
        ext_ref[rows, LATENT:] = rope.astype(jnp.bfloat16)
        ext_t_ref[LATENT:, rows] = rope.T[:ROPE].astype(jnp.bfloat16)
    for load in loads[3:]:
        load.wait()
    for h in range(heads):
        lanes = slice(h * NOPE, (h + 1) * NOPE)
        rows = slice(h * queries, (h + 1) * queries)
        back_ref[rows, :] = dot(grad[:, lanes], up_value[:, lanes]).astype(jnp.bfloat16)
        back_t_ref[:, rows] = dot(up_value[:, lanes], grad[:, lanes]).astype(jnp.bfloat16)


def project(scales, query_nope, query_rope, up_key, up_value, grad_out):
    queries = query_nope.shape[0]
    heads = up_key.shape[1] // NOPE
    rows = heads * queries
    vmem = pl.BlockSpec(memory_space=pltpu.VMEM)
    any_place = pl.BlockSpec(memory_space=pl.ANY)
    operands = (query_nope, query_rope, up_key, up_value, grad_out)
    return pl.pallas_call(
        project_kernel,
        out_shape=(
            jax.ShapeDtypeStruct((rows, PADDED), jnp.bfloat16),
            jax.ShapeDtypeStruct((rows, LATENT), jnp.bfloat16),
            jax.ShapeDtypeStruct((WIDTH, rows), jnp.bfloat16),
            jax.ShapeDtypeStruct((LATENT, rows), jnp.bfloat16),
        ),
        in_specs=[vmem] + [any_place] * len(operands),
        scratch_shapes=[pltpu.VMEM(array.shape, array.dtype) for array in operands]
        + [pltpu.SemaphoreType.DMA((len(operands),))],
        compiler_params=pltpu.CompilerParams(vmem_limit_bytes=58 * 2**20),
        cost_estimate=pl.CostEstimate(flops=8 * rows * NOPE * LATENT, bytes_accessed=7_500_000, transcendentals=0),
        name="project",
    )(scales, *operands)


def fill_cache(cache, blocks, place, core, sems):
    parts = len(blocks) // 2
    half, height = blocks[1].shape[:2]
    copies = []
    for i, block in enumerate(blocks):
        which = core if i < parts else 1 - core
        parity = (place + (i % parts > 0)) % 2
        owners = ((0, 2 * half), (0, half), (half, half))[i % parts]
        start = pl.multiple_of((2 * parity + which) * height, 16)
        copy = pltpu.make_async_copy(block, cache.at[pl.ds(*owners), pl.ds(start, height), :], sems.at[i])
        copy.start()
        copies.append(copy)
    return copies


def keys_of(cache, first, count, features):
    return jnp.concatenate([cache[s, :features, :] for s in range(first, first + count)], axis=1)


def attend_kernel(place_ref, offsets_ref, *refs):
    blocks_hbm, refs = refs[:6], refs[6:]
    (ext_hbm, back_hbm, ext_t_hbm, back_t_hbm), outs_hbm, (ds_hbm, cache_hbm), refs = refs[:4], refs[4:12], refs[12:14], refs[14:]
    (ext, back, ext_t, back_t, cache, bias, score, dprob, acc, ds, outs,
     block_sems, in_sems, ds_sems, out_sems) = refs
    slices = len(outs_hbm) // 2
    height = outs_hbm[0].shape[1]
    place, core = place_ref[0], place_ref[1]
    owners = cache.shape[0]
    keys_total = owners * LANES
    rows_total = ext.shape[0]
    scale = (NOPE + ROPE) ** (-0.5)
    block_loads = fill_cache(cache, blocks_hbm, place, core, block_sems)
    loads = [
        pltpu.make_async_copy(src, dst, in_sems.at[i])
        for i, (src, dst) in enumerate(
            ((ext_hbm, ext), (back_hbm, back), (back_t_hbm, back_t), (ext_t_hbm, ext_t)))
    ]
    loads[0].start()

    queries = bias.shape[0]
    row = lax.broadcasted_iota(jnp.int32, (queries, keys_total), 0)
    key = lax.broadcasted_iota(jnp.int32, (queries, keys_total), 1)
    last = row % QBLOCK + jnp.where(row < QBLOCK, offsets_ref[0], offsets_ref[1])
    bias[...] = jnp.where(key <= last, 0.0, UNSEEN)
    cache[:, WIDTH:, :] = jnp.zeros((owners, PADDED - WIDTH, LANES), jnp.bfloat16)
    for load in block_loads:
        load.wait()
    loads[0].wait()
    for load in loads[1:]:
        load.start()

    tiles = keys_total // KTILE
    per_tile = KTILE // LANES
    rows = rows_total // GROUPS

    def fold(values, op):
        parts = [values[:, k : k + LANES] for k in range(0, KTILE, LANES)]
        return functools.reduce(op, parts)

    def span(g, t):
        return slice(g * rows, (g + 1) * rows), slice(t * KTILE, (t + 1) * KTILE)

    tops = [jnp.full((rows, LANES), UNSEEN, jnp.float32)] * GROUPS
    totals = [jnp.zeros((rows, LANES), jnp.float32)] * GROUPS
    deltas = [jnp.zeros((rows, LANES), jnp.float32)] * GROUPS

    def scores(g, t):
        own, keys = span(g, t)
        mine = keys_of(cache, t * per_tile, per_tile, PADDED)
        raw = jnp.dot(ext[own, :], mine, preferred_element_type=jnp.float32)
        seen = jnp.concatenate([bias[:, keys]] * (rows // queries), axis=0)
        raw = raw * (scale * LOG2E) + seen
        score[own, keys] = raw
        tops[g] = jnp.maximum(tops[g], fold(raw, jnp.maximum))
        if g == 0 and t == 0:
            loads[1].wait()
        dprob[own, keys] = jnp.dot(back[own, :], mine[:LATENT], preferred_element_type=jnp.float32)
        if t == tiles - 1:
            tops[g] = jnp.max(tops[g], axis=1, keepdims=True)

    def weights(g, t):
        own, keys = span(g, t)
        weight = jnp.exp2(score[own, keys] - tops[g])
        score[own, keys] = weight
        totals[g] = totals[g] + fold(weight, jnp.add)
        if t == tiles - 1:
            totals[g] = 1.0 / jnp.sum(totals[g], axis=1, keepdims=True)

    def values(g, t):
        own, keys = span(g, t)
        probs = (score[own, keys] * totals[g]).astype(jnp.bfloat16)
        part = jnp.dot(back_t[:, own], probs, preferred_element_type=jnp.float32)
        if g == 0:
            acc[:LATENT, keys] = part
        else:
            acc[:LATENT, keys] += part
        deltas[g] = deltas[g] + fold(probs.astype(jnp.float32) * dprob[own, keys], jnp.add)
        if t == tiles - 1:
            deltas[g] = jnp.sum(deltas[g], axis=1, keepdims=True)

    stores = [pltpu.make_async_copy(cache, cache_hbm, block_sems.at[len(blocks_hbm)])]
    stores[0].start()

    def gradients(g, t):
        own, keys = span(g, t)
        dscore = score[own, keys] * (totals[g] * scale) * (dprob[own, keys] - deltas[g])
        dscore = dscore.astype(jnp.bfloat16)
        ds[own, keys] = dscore
        store = pltpu.make_async_copy(ds.at[own, keys], ds_hbm.at[own, keys], ds_sems.at[g, t])
        store.start()
        stores.append(store)
        part = jnp.dot(ext_t[:, own], dscore, preferred_element_type=jnp.float32)
        acc[:LATENT, keys] += part[:LATENT]
        if g == 0:
            acc[LATENT:, keys] = part[LATENT:]
        else:
            acc[LATENT:, keys] += part[LATENT:]

    def put_out(t):
        mine = slice(t * per_tile, (t + 1) * per_tile)
        for s in range(t * per_tile, (t + 1) * per_tile):
            outs[s] = acc[:, s * LANES : (s + 1) * LANES].astype(jnp.bfloat16)
        for i, out in enumerate(outs_hbm):
            which = core if i < slices else 1 - core
            start = pl.multiple_of((2 * ((place + i) % slices) + which) * height, 8)
            store = pltpu.make_async_copy(outs.at[mine, pl.ds(start, height), :], out.at[mine], out_sems.at[i, t])
            store.start()
            stores.append(store)

    stages = (scores, weights, values, gradients)
    for step in range(len(stages) + GROUPS - 1):
        if step == stages.index(values):
            loads[2].wait()
            loads[3].wait()
        for t in range(tiles):
            for g in range(GROUPS):
                if 0 <= step - g < len(stages):
                    stages[step - g](g, t)
            if step == len(stages) + GROUPS - 2:
                put_out(t)
    for store in stores:
        store.wait()


def attend(slices, place, offsets, blocks, ext, back, ext_t, back_t):
    rows = ext.shape[0]
    owners = blocks[0].shape[0]
    height = WIDTH // (2 * slices)
    keys_total = owners * LANES
    queries = offsets.shape[0] * QBLOCK
    tiles = keys_total // KTILE
    smem = pl.BlockSpec(memory_space=pltpu.SMEM)
    any_place = pl.BlockSpec(memory_space=pl.ANY)
    bf16, f32 = jnp.bfloat16, jnp.float32
    sums = 2 * slices
    *outs, dscore, whole = pl.pallas_call(
        attend_kernel,
        out_shape=[jax.ShapeDtypeStruct((owners, height, LANES), bf16)] * sums
        + [jax.ShapeDtypeStruct((rows, keys_total), bf16), jax.ShapeDtypeStruct((owners, PADDED, LANES), bf16)],
        in_specs=[smem, smem] + [any_place] * (len(blocks) + 4),
        out_specs=[any_place] * (sums + 2),
        scratch_shapes=[
            pltpu.VMEM(ext.shape, bf16),
            pltpu.VMEM(back.shape, bf16),
            pltpu.VMEM(ext_t.shape, bf16),
            pltpu.VMEM(back_t.shape, bf16),
            pltpu.VMEM((owners, PADDED, LANES), bf16),
            pltpu.VMEM((queries, keys_total), f32),
            pltpu.VMEM((rows, keys_total), f32),
            pltpu.VMEM((rows, keys_total), f32),
            pltpu.VMEM((WIDTH, keys_total), f32),
            pltpu.VMEM((rows, keys_total), bf16),
            pltpu.VMEM((owners, WIDTH, LANES), bf16),
            pltpu.SemaphoreType.DMA((len(blocks) + 1,)),
            pltpu.SemaphoreType.DMA((4,)),
            pltpu.SemaphoreType.DMA((GROUPS, tiles)),
            pltpu.SemaphoreType.DMA((sums, tiles)),
        ],
        compiler_params=pltpu.CompilerParams(vmem_limit_bytes=VMEM),
        cost_estimate=pl.CostEstimate(
            flops=2 * rows * keys_total * (2 * PADDED + 2 * LATENT),
            bytes_accessed=14_000_000, transcendentals=rows * keys_total),
        name="attend",
    )(place, offsets, *blocks, ext, back, ext_t, back_t)
    return outs[: sums // 2], outs[sums // 2 :], dscore, whole


def query_kernel(first, ready, scale_ref, ds_hbm, cache_hbm, key_hbm, *refs):
    nope_hbm, rope_hbm, ds, up_key, parts, cache, grad_buf, nope, rope_out, sems = refs[2 * ready :]
    queries = nope.shape[0]
    count = ds.shape[0] // queries
    half = ds.shape[0] // 2
    start = first * queries
    heads = up_key.shape[1] // NOPE
    loads = [
        pltpu.make_async_copy(cache_hbm, parts, sems.at[0]),
        pltpu.make_async_copy(ds_hbm.at[start : start + half], ds.at[:half], sems.at[1]),
        pltpu.make_async_copy(ds_hbm.at[start + half : start + 2 * half], ds.at[half:], sems.at[2]),
        pltpu.make_async_copy(key_hbm.at[:, first * NOPE : (first + count) * NOPE], up_key, sems.at[3]),
    ]
    for load in loads:
        load.start()
    factor = jnp.exp2(scale_ref[...].astype(jnp.float32))
    loads[0].wait()
    cache[...] = keys_of(parts, 0, parts.shape[0], PADDED)
    for i in range(2):
        own = slice(i * half, (i + 1) * half)
        loads[1 + i].wait()
        grad_buf[own, :] = lax.dot_general(ds[own, :], cache[...], COLS, preferred_element_type=jnp.float32)
    loads[3].wait()
    for h in range(heads):
        lanes = slice(h * NOPE, (h + 1) * NOPE)
        grad = grad_buf[h * queries : (h + 1) * queries, :]
        part = jnp.dot(grad[:, :LATENT].astype(jnp.bfloat16), up_key[:, lanes], preferred_element_type=jnp.float32)
        nope[:, lanes] = (part * factor).astype(jnp.bfloat16)
        rope = grad[:, LATENT:] * factor
        if h % 2 == 0:
            even = rope
        else:
            pair = slice(h // 2 * LANES, (h // 2 + 1) * LANES)
            rope_out[:, pair] = (even + pltpu.roll(rope, ROPE, 1)).astype(jnp.bfloat16)
    stores = [
        pltpu.make_async_copy(nope, nope_hbm.at[:, first * NOPE : (first + count) * NOPE], sems.at[4]),
        pltpu.make_async_copy(rope_out, rope_hbm.at[:, first * ROPE : (first + count) * ROPE], sems.at[5]),
    ]
    for store in stores:
        store.start()
    for store in stores:
        store.wait()


def query_gradients(first, count, scales, dscore, whole, up_key, ready=()):
    keys_total = dscore.shape[1]
    heads = up_key.shape[1] // NOPE
    queries = scales.shape[0]
    rows = count * queries
    vmem = pl.BlockSpec(memory_space=pltpu.VMEM)
    any_place = pl.BlockSpec(memory_space=pl.ANY)
    bf16, f32 = jnp.bfloat16, jnp.float32
    return pl.pallas_call(
        functools.partial(query_kernel, first, len(ready) // 2),
        out_shape=(
            jax.ShapeDtypeStruct((queries, heads * NOPE), bf16),
            jax.ShapeDtypeStruct((queries, heads * ROPE), bf16),
        ),
        in_specs=[vmem] + [any_place] * (3 + len(ready)),
        out_specs=(any_place, any_place),
        scratch_shapes=[
            pltpu.VMEM((rows, keys_total), bf16),
            pltpu.VMEM((up_key.shape[0], count * NOPE), bf16),
            pltpu.VMEM(whole.shape, bf16),
            pltpu.VMEM((PADDED, keys_total), bf16),
            pltpu.VMEM((rows, PADDED), f32),
            pltpu.VMEM((queries, count * NOPE), bf16),
            pltpu.VMEM((queries, count * ROPE), bf16),
            pltpu.SemaphoreType.DMA((6,)),
        ],
        input_output_aliases={4 + i: i for i in range(len(ready))},
        compiler_params=pltpu.CompilerParams(vmem_limit_bytes=58 * 2**20),
        cost_estimate=pl.CostEstimate(
            flops=2 * rows * keys_total * PADDED, bytes_accessed=9_000_000, transcendentals=0),
        name=f"query_gradients_{first}",
    )(scales, dscore, whole, up_key, *ready)


def per_device(cache, query_nope, query_rope, scale_exp, offsets, up_key, up_value, grad_out):
    place = jnp.stack([lax.axis_index("x"), lax.axis_index("core")]).astype(jnp.int32)
    own = place[0] % 2 * 2 + place[1]
    height = WIDTH // 4
    mine = lax.dynamic_slice_in_dim(cache.T, own * height, height, 0)
    scales = scale_exp.reshape(-1, 1)
    projected = project(scales, query_nope, query_rope, up_key, up_value, grad_out)
    over_seq, projected = lax.optimization_barrier((to_each(mine, SEQ), projected))
    here = gather_over_x(over_seq)
    blocks = here + [swap_core(block) for block in here]
    keeps, sends, dscore, whole = attend(lax.axis_size("x"), place, offsets, blocks, *projected)
    slices = reduce_over_x(*core_sums(keeps, sends))
    part = up_key.shape[1] // NOPE // 2
    early = query_gradients(0, part, scales, dscore, whole, up_key)
    slices, early = lax.optimization_barrier((slices, early))
    query_grads = query_gradients(part, part, scales, dscore, whole, up_key, early)
    slices = add_up(lax.all_to_all(slices, SEQ, 0, 0, tiled=True))
    slices, query_grads = lax.optimization_barrier((slices, query_grads))
    return (owned_columns(slices), *query_grads)


def solution(mesh):
    wide = Mesh(mesh.devices.reshape(8, 2, 4, 2, 2), SEQ + HEAD)
    in_specs = (
        P(SEQ, None),
        P(SEQ, HEAD),
        P(SEQ, HEAD),
        P(SEQ),
        P(SEQ),
        P(None, HEAD),
        P(None, HEAD),
        P(SEQ, HEAD),
    )
    out_specs = (P(SEQ, None), P(SEQ, HEAD), P(SEQ, HEAD))
    return jax.shard_map(per_device, mesh=wide, in_specs=in_specs, out_specs=out_specs, check_vma=False)
```

```python
import functools

import jax
import jax.numpy as jnp
from jax import lax
from jax.experimental import pallas as pl
from jax.experimental.pallas import tpu as pltpu
from jax.sharding import Mesh, PartitionSpec as P

LATENT = 512
ROPE = 64
NOPE = 128
QBLOCK = 64
WIDTH = LATENT + ROPE
LANES = 128
PADDED = LATENT + LANES
KTILE = 1024
GROUPS = 1
VMEM = 49 * 2**20
LOG2E = 1.4426950408889634
UNSEEN = -1e30
SEQ = ("z", "y_lo")
HEAD = ("x", "y_hi", "core")
COLS = (((1,), (1,)), ((), ()))


def to_each(block, axes):
    copies = jnp.broadcast_to(block, (lax.axis_size(axes), *block.shape))
    return lax.all_to_all(copies, axes, 0, 0, tiled=True)


def swap_core(block):
    return lax.ppermute(block, "core", [(0, 1), (1, 0)])


def add_up(blocks):
    return jnp.sum(blocks.astype(jnp.float32), axis=0).astype(jnp.bfloat16)


def to_next(block):
    size = lax.axis_size("x")
    return lax.ppermute(block, "x", [(i, (i + 1) % size) for i in range(size)])


def to_previous(block):
    size = lax.axis_size("x")
    return lax.ppermute(block, "x", [(i, (i - 1) % size) for i in range(size)])


def to_side(block):
    size = lax.axis_size("x")
    pairs = [(2 * i + c, 2 * ((i + (-1 if c else 1)) % size) + c) for i in range(size) for c in range(2)]
    return lax.ppermute(block, ("x", "core"), pairs)


def gather_over_x(block):
    half = block.shape[0] // 2
    return [block, to_previous(block[:half]), to_next(block[half:])]


def reduce_over_x(own, after, far, before):
    first = lax.axis_index("core") == 0
    passed = to_side(far.astype(jnp.bfloat16)).astype(jnp.float32)
    after = to_next((after + jnp.where(first, passed, 0.0)).astype(jnp.bfloat16))
    before = to_previous((before + jnp.where(first, 0.0, passed)).astype(jnp.bfloat16))
    return (own + after.astype(jnp.float32) + before.astype(jnp.float32)).astype(jnp.bfloat16)


def core_sums(keeps, sends):
    sums = [None] * 4
    for i in (2, 1, 3, 0):
        sums[i] = keeps[i].astype(jnp.float32) + swap_core(sends[i]).astype(jnp.float32)
    return sums


def owned_columns(slices):
    parts = to_each(slices, HEAD)
    sizes = [lax.axis_size(axis) for axis in HEAD]
    parts = parts.reshape(*sizes, *slices.shape).astype(jnp.float32)
    parts = jnp.sum(parts, axis=1).astype(jnp.bfloat16)
    return parts.reshape(-1, slices.shape[-1]).T


def project_kernel(scale_ref, nope_hbm, rope_hbm, key_hbm, value_hbm, grad_hbm, ext_ref, back_ref, ext_t_ref, back_t_ref,
                   nope, rope_in, up_key, up_value, grad, sems):
    queries = nope.shape[0]
    heads = up_key.shape[1] // NOPE
    loads = [
        pltpu.make_async_copy(src, dst, sems.at[i])
        for i, (src, dst) in enumerate(
            ((nope_hbm, nope), (key_hbm, up_key), (rope_hbm, rope_in), (grad_hbm, grad), (value_hbm, up_value)))
    ]
    for load in loads:
        load.start()
    factor = jnp.exp2(scale_ref[...].astype(jnp.float32))
    dot = functools.partial(lax.dot_general, dimension_numbers=COLS, preferred_element_type=jnp.float32)
    lane = lax.broadcasted_iota(jnp.int32, (queries, LANES), 1)
    for load in loads[:3]:
        load.wait()
    for h in range(heads):
        lanes = slice(h * NOPE, (h + 1) * NOPE)
        rows = slice(h * queries, (h + 1) * queries)
        q_nope = (nope[:, lanes].astype(jnp.float32) * factor).astype(jnp.bfloat16)
        ext_ref[rows, :LATENT] = dot(q_nope, up_key[:, lanes]).astype(jnp.bfloat16)
        ext_t_ref[:LATENT, rows] = dot(up_key[:, lanes], q_nope).astype(jnp.bfloat16)
        pair = slice(h // 2 * LANES, (h // 2 + 1) * LANES)
        rope = rope_in[:, pair].astype(jnp.float32) * factor
        if h % 2:
            rope = pltpu.roll(rope, ROPE, 1)
        rope = jnp.where(lane < ROPE, rope, 0.0)
        ext_ref[rows, LATENT:] = rope.astype(jnp.bfloat16)
        ext_t_ref[LATENT:, rows] = rope.T[:ROPE].astype(jnp.bfloat16)
    for load in loads[3:]:
        load.wait()
    for h in range(heads):
        lanes = slice(h * NOPE, (h + 1) * NOPE)
        rows = slice(h * queries, (h + 1) * queries)
        back_ref[rows, :] = dot(grad[:, lanes], up_value[:, lanes]).astype(jnp.bfloat16)
        back_t_ref[:, rows] = dot(up_value[:, lanes], grad[:, lanes]).astype(jnp.bfloat16)


def project(scales, query_nope, query_rope, up_key, up_value, grad_out):
    queries = query_nope.shape[0]
    heads = up_key.shape[1] // NOPE
    rows = heads * queries
    vmem = pl.BlockSpec(memory_space=pltpu.VMEM)
    any_place = pl.BlockSpec(memory_space=pl.ANY)
    operands = (query_nope, query_rope, up_key, up_value, grad_out)
    return pl.pallas_call(
        project_kernel,
        out_shape=(
            jax.ShapeDtypeStruct((rows, PADDED), jnp.bfloat16),
            jax.ShapeDtypeStruct((rows, LATENT), jnp.bfloat16),
            jax.ShapeDtypeStruct((WIDTH, rows), jnp.bfloat16),
            jax.ShapeDtypeStruct((LATENT, rows), jnp.bfloat16),
        ),
        in_specs=[vmem] + [any_place] * len(operands),
        scratch_shapes=[pltpu.VMEM(array.shape, array.dtype) for array in operands]
        + [pltpu.SemaphoreType.DMA((len(operands),))],
        compiler_params=pltpu.CompilerParams(vmem_limit_bytes=58 * 2**20),
        cost_estimate=pl.CostEstimate(flops=8 * rows * NOPE * LATENT, bytes_accessed=7_500_000, transcendentals=0),
        name="project",
    )(scales, *operands)


def fill_cache(cache, blocks, place, core, sems):
    parts = len(blocks) // 2
    half, height = blocks[1].shape[:2]
    copies = []
    for i, block in enumerate(blocks):
        which = core if i < parts else 1 - core
        parity = (place + (i % parts > 0)) % 2
        owners = ((0, 2 * half), (0, half), (half, half))[i % parts]
        start = pl.multiple_of((2 * parity + which) * height, 16)
        copy = pltpu.make_async_copy(block, cache.at[pl.ds(*owners), pl.ds(start, height), :], sems.at[i])
        copy.start()
        copies.append(copy)
    return copies


def keys_of(cache, first, count, features):
    return jnp.concatenate([cache[s, :features, :] for s in range(first, first + count)], axis=1)


def attend_kernel(place_ref, offsets_ref, *refs):
    blocks_hbm, refs = refs[:6], refs[6:]
    (ext_hbm, back_hbm, ext_t_hbm, back_t_hbm), outs_hbm, (ds_hbm, cache_hbm), refs = refs[:4], refs[4:12], refs[12:14], refs[14:]
    (ext, back, ext_t, back_t, cache, bias, score, dprob, acc, ds, outs,
     block_sems, in_sems, ds_sems, out_sems) = refs
    slices = len(outs_hbm) // 2
    height = outs_hbm[0].shape[1]
    place, core = place_ref[0], place_ref[1]
    owners = cache.shape[0]
    keys_total = owners * LANES
    rows_total = ext.shape[0]
    scale = (NOPE + ROPE) ** (-0.5)
    block_loads = fill_cache(cache, blocks_hbm, place, core, block_sems)
    loads = [
        pltpu.make_async_copy(src, dst, in_sems.at[i])
        for i, (src, dst) in enumerate(
            ((ext_hbm, ext), (back_hbm, back), (back_t_hbm, back_t), (ext_t_hbm, ext_t)))
    ]
    loads[0].start()

    queries = bias.shape[0]
    row = lax.broadcasted_iota(jnp.int32, (queries, keys_total), 0)
    key = lax.broadcasted_iota(jnp.int32, (queries, keys_total), 1)
    last = row % QBLOCK + jnp.where(row < QBLOCK, offsets_ref[0], offsets_ref[1])
    bias[...] = jnp.where(key <= last, 0.0, UNSEEN)
    cache[:, WIDTH:, :] = jnp.zeros((owners, PADDED - WIDTH, LANES), jnp.bfloat16)
    for load in block_loads:
        load.wait()
    loads[0].wait()
    for load in loads[1:]:
        load.start()

    tiles = keys_total // KTILE
    per_tile = KTILE // LANES
    rows = rows_total // GROUPS

    def fold(values, op):
        parts = [values[:, k : k + LANES] for k in range(0, KTILE, LANES)]
        return functools.reduce(op, parts)

    def span(g, t):
        return slice(g * rows, (g + 1) * rows), slice(t * KTILE, (t + 1) * KTILE)

    tops = [jnp.full((rows, LANES), UNSEEN, jnp.float32)] * GROUPS
    totals = [jnp.zeros((rows, LANES), jnp.float32)] * GROUPS
    deltas = [jnp.zeros((rows, LANES), jnp.float32)] * GROUPS

    def scores(g, t):
        own, keys = span(g, t)
        mine = keys_of(cache, t * per_tile, per_tile, PADDED)
        raw = jnp.dot(ext[own, :], mine, preferred_element_type=jnp.float32)
        seen = jnp.concatenate([bias[:, keys]] * (rows // queries), axis=0)
        raw = raw * (scale * LOG2E) + seen
        score[own, keys] = raw
        tops[g] = jnp.maximum(tops[g], fold(raw, jnp.maximum))
        if g == 0 and t == 0:
            loads[1].wait()
        dprob[own, keys] = jnp.dot(back[own, :], mine[:LATENT], preferred_element_type=jnp.float32)
        if t == tiles - 1:
            tops[g] = jnp.max(tops[g], axis=1, keepdims=True)

    def weights(g, t):
        own, keys = span(g, t)
        weight = jnp.exp2(score[own, keys] - tops[g])
        score[own, keys] = weight
        totals[g] = totals[g] + fold(weight, jnp.add)
        if t == tiles - 1:
            totals[g] = 1.0 / jnp.sum(totals[g], axis=1, keepdims=True)

    def values(g, t):
        own, keys = span(g, t)
        probs = (score[own, keys] * totals[g]).astype(jnp.bfloat16)
        part = jnp.dot(back_t[:, own], probs, preferred_element_type=jnp.float32)
        if g == 0:
            acc[:LATENT, keys] = part
        else:
            acc[:LATENT, keys] += part
        deltas[g] = deltas[g] + fold(probs.astype(jnp.float32) * dprob[own, keys], jnp.add)
        if t == tiles - 1:
            deltas[g] = jnp.sum(deltas[g], axis=1, keepdims=True)

    stores = [pltpu.make_async_copy(cache, cache_hbm, block_sems.at[len(blocks_hbm)])]
    stores[0].start()

    def gradients(g, t):
        own, keys = span(g, t)
        dscore = score[own, keys] * (totals[g] * scale) * (dprob[own, keys] - deltas[g])
        dscore = dscore.astype(jnp.bfloat16)
        ds[own, keys] = dscore
        store = pltpu.make_async_copy(ds.at[own, keys], ds_hbm.at[own, keys], ds_sems.at[g, t])
        store.start()
        stores.append(store)
        part = jnp.dot(ext_t[:, own], dscore, preferred_element_type=jnp.float32)
        acc[:LATENT, keys] += part[:LATENT]
        if g == 0:
            acc[LATENT:, keys] = part[LATENT:]
        else:
            acc[LATENT:, keys] += part[LATENT:]

    def put_out(t):
        mine = slice(t * per_tile, (t + 1) * per_tile)
        for s in range(t * per_tile, (t + 1) * per_tile):
            outs[s] = acc[:, s * LANES : (s + 1) * LANES].astype(jnp.bfloat16)
        for i, out in enumerate(outs_hbm):
            which = core if i < slices else 1 - core
            start = pl.multiple_of((2 * ((place + i) % slices) + which) * height, 8)
            store = pltpu.make_async_copy(outs.at[mine, pl.ds(start, height), :], out.at[mine], out_sems.at[i, t])
            store.start()
            stores.append(store)

    stages = (scores, weights, values, gradients)
    for step in range(len(stages) + GROUPS - 1):
        if step == stages.index(values):
            loads[2].wait()
            loads[3].wait()
        for t in range(tiles):
            for g in range(GROUPS):
                if 0 <= step - g < len(stages):
                    stages[step - g](g, t)
            if step == len(stages) + GROUPS - 2:
                put_out(t)
    for store in stores:
        store.wait()


def attend(slices, place, offsets, blocks, ext, back, ext_t, back_t):
    rows = ext.shape[0]
    owners = blocks[0].shape[0]
    height = WIDTH // (2 * slices)
    keys_total = owners * LANES
    queries = offsets.shape[0] * QBLOCK
    tiles = keys_total // KTILE
    smem = pl.BlockSpec(memory_space=pltpu.SMEM)
    any_place = pl.BlockSpec(memory_space=pl.ANY)
    bf16, f32 = jnp.bfloat16, jnp.float32
    sums = 2 * slices
    *outs, dscore, whole = pl.pallas_call(
        attend_kernel,
        out_shape=[jax.ShapeDtypeStruct((owners, height, LANES), bf16)] * sums
        + [jax.ShapeDtypeStruct((rows, keys_total), bf16), jax.ShapeDtypeStruct((owners, PADDED, LANES), bf16)],
        in_specs=[smem, smem] + [any_place] * (len(blocks) + 4),
        out_specs=[any_place] * (sums + 2),
        scratch_shapes=[
            pltpu.VMEM(ext.shape, bf16),
            pltpu.VMEM(back.shape, bf16),
            pltpu.VMEM(ext_t.shape, bf16),
            pltpu.VMEM(back_t.shape, bf16),
            pltpu.VMEM((owners, PADDED, LANES), bf16),
            pltpu.VMEM((queries, keys_total), f32),
            pltpu.VMEM((rows, keys_total), f32),
            pltpu.VMEM((rows, keys_total), f32),
            pltpu.VMEM((WIDTH, keys_total), f32),
            pltpu.VMEM((rows, keys_total), bf16),
            pltpu.VMEM((owners, WIDTH, LANES), bf16),
            pltpu.SemaphoreType.DMA((len(blocks) + 1,)),
            pltpu.SemaphoreType.DMA((4,)),
            pltpu.SemaphoreType.DMA((GROUPS, tiles)),
            pltpu.SemaphoreType.DMA((sums, tiles)),
        ],
        compiler_params=pltpu.CompilerParams(vmem_limit_bytes=VMEM),
        cost_estimate=pl.CostEstimate(
            flops=2 * rows * keys_total * (2 * PADDED + 2 * LATENT),
            bytes_accessed=14_000_000, transcendentals=rows * keys_total),
        name="attend",
    )(place, offsets, *blocks, ext, back, ext_t, back_t)
    return outs[: sums // 2], outs[sums // 2 :], dscore, whole


def query_kernel(first, ready, scale_ref, ds_hbm, cache_hbm, key_hbm, *refs):
    nope_hbm, rope_hbm, ds, up_key, parts, cache, grad_buf, nope, rope_out, sems = refs[2 * ready :]
    queries = nope.shape[0]
    count = ds.shape[0] // queries
    half = ds.shape[0] // 2
    start = first * queries
    heads = up_key.shape[1] // NOPE
    loads = [
        pltpu.make_async_copy(cache_hbm, parts, sems.at[0]),
        pltpu.make_async_copy(ds_hbm.at[start : start + half], ds.at[:half], sems.at[1]),
        pltpu.make_async_copy(ds_hbm.at[start + half : start + 2 * half], ds.at[half:], sems.at[2]),
        pltpu.make_async_copy(key_hbm.at[:, first * NOPE : (first + count) * NOPE], up_key, sems.at[3]),
    ]
    for load in loads:
        load.start()
    factor = jnp.exp2(scale_ref[...].astype(jnp.float32))
    loads[0].wait()
    cache[...] = keys_of(parts, 0, parts.shape[0], PADDED)
    for i in range(2):
        own = slice(i * half, (i + 1) * half)
        loads[1 + i].wait()
        grad_buf[own, :] = lax.dot_general(ds[own, :], cache[...], COLS, preferred_element_type=jnp.float32)
    loads[3].wait()
    for h in range(heads):
        lanes = slice(h * NOPE, (h + 1) * NOPE)
        grad = grad_buf[h * queries : (h + 1) * queries, :]
        part = jnp.dot(grad[:, :LATENT].astype(jnp.bfloat16), up_key[:, lanes], preferred_element_type=jnp.float32)
        nope[:, lanes] = (part * factor).astype(jnp.bfloat16)
        rope = grad[:, LATENT:] * factor
        if h % 2 == 0:
            even = rope
        else:
            pair = slice(h // 2 * LANES, (h // 2 + 1) * LANES)
            rope_out[:, pair] = (even + pltpu.roll(rope, ROPE, 1)).astype(jnp.bfloat16)
    stores = [
        pltpu.make_async_copy(nope, nope_hbm.at[:, first * NOPE : (first + count) * NOPE], sems.at[4]),
        pltpu.make_async_copy(rope_out, rope_hbm.at[:, first * ROPE : (first + count) * ROPE], sems.at[5]),
    ]
    for store in stores:
        store.start()
    for store in stores:
        store.wait()


def query_gradients(first, count, scales, dscore, whole, up_key, ready=()):
    keys_total = dscore.shape[1]
    heads = up_key.shape[1] // NOPE
    queries = scales.shape[0]
    rows = count * queries
    vmem = pl.BlockSpec(memory_space=pltpu.VMEM)
    any_place = pl.BlockSpec(memory_space=pl.ANY)
    bf16, f32 = jnp.bfloat16, jnp.float32
    return pl.pallas_call(
        functools.partial(query_kernel, first, len(ready) // 2),
        out_shape=(
            jax.ShapeDtypeStruct((queries, heads * NOPE), bf16),
            jax.ShapeDtypeStruct((queries, heads * ROPE), bf16),
        ),
        in_specs=[vmem] + [any_place] * (3 + len(ready)),
        out_specs=(any_place, any_place),
        scratch_shapes=[
            pltpu.VMEM((rows, keys_total), bf16),
            pltpu.VMEM((up_key.shape[0], count * NOPE), bf16),
            pltpu.VMEM(whole.shape, bf16),
            pltpu.VMEM((PADDED, keys_total), bf16),
            pltpu.VMEM((rows, PADDED), f32),
            pltpu.VMEM((queries, count * NOPE), bf16),
            pltpu.VMEM((queries, count * ROPE), bf16),
            pltpu.SemaphoreType.DMA((6,)),
        ],
        input_output_aliases={4 + i: i for i in range(len(ready))},
        compiler_params=pltpu.CompilerParams(vmem_limit_bytes=58 * 2**20),
        cost_estimate=pl.CostEstimate(
            flops=2 * rows * keys_total * PADDED, bytes_accessed=9_000_000, transcendentals=0),
        name=f"query_gradients_{first}",
    )(scales, dscore, whole, up_key, *ready)


def per_device(cache, query_nope, query_rope, scale_exp, offsets, up_key, up_value, grad_out):
    place = jnp.stack([lax.axis_index("x"), lax.axis_index("core")]).astype(jnp.int32)
    own = place[0] % 2 * 2 + place[1]
    height = WIDTH // 4
    mine = lax.dynamic_slice_in_dim(cache.T, own * height, height, 0)
    scales = scale_exp.reshape(-1, 1)
    projected = project(scales, query_nope, query_rope, up_key, up_value, grad_out)
    over_seq, projected = lax.optimization_barrier((to_each(mine, SEQ), projected))
    here = gather_over_x(over_seq)
    blocks = here + [swap_core(block) for block in here]
    keeps, sends, dscore, whole = attend(lax.axis_size("x"), place, offsets, blocks, *projected)
    slices = reduce_over_x(*core_sums(keeps, sends))
    part = up_key.shape[1] // NOPE // 2
    early = query_gradients(0, part, scales, dscore, whole, up_key)
    slices, early = lax.optimization_barrier((slices, early))
    slices = add_up(lax.all_to_all(slices, SEQ, 0, 0, tiled=True))
    slices, early = lax.optimization_barrier((slices, early))
    query_grads = query_gradients(part, part, scales, dscore, whole, up_key, early)
    return (owned_columns(slices), *query_grads)


def solution(mesh):
    wide = Mesh(mesh.devices.reshape(8, 2, 4, 2, 2), SEQ + HEAD)
    in_specs = (
        P(SEQ, None),
        P(SEQ, HEAD),
        P(SEQ, HEAD),
        P(SEQ),
        P(SEQ),
        P(None, HEAD),
        P(None, HEAD),
        P(SEQ, HEAD),
    )
    out_specs = (P(SEQ, None), P(SEQ, HEAD), P(SEQ, HEAD))
    return jax.shard_map(per_device, mesh=wide, in_specs=in_specs, out_specs=out_specs, check_vma=False)
```
